512 devices in a mesh: patch: 512 (over y, x, z, core).
Axes of the slice: x: 4, y: 4, z: 16, core: 2. Of those that a mesh axis runs over, the one named last changes fastest.
Arguments:
- fields: float32 [4, 32, 32, 65536], P(None, None, None, 'patch'), may hold values from -1.5 to 4, as said below
- patch_level: int32 [65536], P('patch'), may hold values from 4 to 6
- relation: int32 [65536, 4], P('patch'), may hold values from 0 to 3
- face_half: int32 [65536, 4], P('patch'), may hold values from 0 to 1
- neighbour: int32 [65536, 4, 2], P('patch'), may hold values from 0 to 255, as said below
- send_list: int32 [512, 16, 8], P('patch'), may hold values from 0 to 127, as said below
Outputs:
- advanced: float32 [4, 32, 32, 65536], P(None, None, None, 'patch')
- time_step: float32 [], replicated
The draws below stay inside these ranges and needn't reach their ends.
Inputs may be any that keep to these rules, and one draw needn't show every extreme that they name: `send_list`: within each device's block for one curve distance the 8 entries are distinct local patches. `neighbour`: A reference of 128 or more names a slot of a device that exists on the curve. The second reference of a face is used only where relation is 3. `fields`: h lies in [2, 4], |hu| and |hv| at most 1.5, hc in [0, h].
All inputs are finite; a program needn't handle non-finite values.
Results may differ from the reference program's by a relative error of at most 0.0003.
Values sent between devices are 32-bit elements; how exact they have to be, the bound alone decides.
A program may use at most 128 MiB of HBM per device.

```python
import jax
import jax.numpy as jnp
from jax import lax

CELLS = 32
HOPS = 8
P_DEV = 128
SEND = 8
NOFF = 16
POOL = 256
PATCHES = 65536
N_PATCH = 512


def draw_fields(key, part):
    keys = jax.random.split(key, 8)
    shape = (CELLS, CELLS, PATCHES)
    depth = jax.random.uniform(keys[1], shape, minval=2.0, maxval=4.0)
    flow_x = 0.5 * jax.random.truncated_normal(keys[3], -3.0, 3.0, shape)
    flow_y = 0.5 * jax.random.truncated_normal(keys[5], -3.0, 3.0, shape)
    tracer = depth * jax.random.uniform(keys[6], shape)
    return jnp.stack([depth, flow_x, flow_y, tracer]).astype(jnp.float32)


def draw_neighbour(key, part):
    keys = jax.random.split(key, 4)
    shape = (PATCHES, 4, 2)
    devices = PATCHES // P_DEV
    owner = (jnp.arange(PATCHES, dtype=jnp.int32) // P_DEV)[:, None, None]
    local = jax.random.randint(keys[0], shape, 0, P_DEV)
    block_index = jax.random.randint(keys[1], shape, 0, NOFF)
    slot = jax.random.randint(keys[2], shape, 0, SEND)
    remote = jax.random.randint(keys[3], shape, 0, 2) == 1
    distance = jnp.where(block_index < HOPS, block_index + 1, HOPS - 1 - block_index)
    source = owner - distance
    usable = remote & (source >= 0) & (source < devices)
    return jnp.where(usable, P_DEV + block_index * SEND + slot, local).astype(jnp.int32)


def draw_send_list(key, part):
    devices = PATCHES // P_DEV
    scores = jax.random.randint(key, (devices, NOFF, P_DEV), 0, 1 << 20) * P_DEV + jnp.arange(P_DEV, dtype=jnp.int32)
    order = jnp.argsort(scores, axis=-1, stable=True)
    return order[..., :SEND].astype(jnp.int32)


def touch_ends(values, rng, low, top_value):
    shape = values.shape
    spot = [jax.random.randint(jax.random.fold_in(rng, axis), (), 0, shape[axis]) for axis in range(len(shape))]
    values = values.at[tuple(spot)].set(low)
    longest = shape.index(max(shape))
    spot[longest] = (spot[longest] + 1) % shape[longest]
    return values.at[tuple(spot)].set(top_value)


def setup_inputs(seed: int = 0) -> dict:
    key_list = jax.random.split(jax.random.key(seed), 7)
    fields = draw_fields(jax.random.fold_in(key_list[6], 71), 0)
    patch_level = touch_ends(jax.random.randint(key_list[1], (PATCHES,), 4, 7), jax.random.fold_in(key_list[1], 1), 4, 6).astype(jnp.int32)
    relation = touch_ends(jax.random.randint(key_list[2], (PATCHES, 4), 0, 4), jax.random.fold_in(key_list[2], 1), 0, 3).astype(jnp.int32)
    face_half = touch_ends(jax.random.randint(key_list[3], (PATCHES, 4), 0, 2), jax.random.fold_in(key_list[3], 1), 0, 1).astype(jnp.int32)
    neighbour = draw_neighbour(jax.random.fold_in(key_list[6], 71), 0)
    send_list = draw_send_list(jax.random.fold_in(key_list[6], 71), 0)
    return dict(fields=fields, patch_level=patch_level, relation=relation, face_half=face_half, neighbour=neighbour, send_list=send_list)


courant = 0.4
finest_level = 6.0

def face_strips(state):
    west_side = state[:, 0:4]
    east_side = state[:, ::-1][:, 0:4]
    south_side = jnp.swapaxes(state[:, :, 0:4], 1, 2)
    north_side = jnp.swapaxes(state[:, :, ::-1][:, :, 0:4], 1, 2)
    stacked = jnp.stack([west_side, east_side, south_side, north_side])
    return jnp.transpose(stacked, (4, 0, 1, 2, 3))

def restrict(strip):
    total = strip[..., 0::2, 0::2] + strip[..., 1::2, 0::2]
    total = total + strip[..., 0::2, 1::2]
    total = total + strip[..., 1::2, 1::2]
    return 0.25 * total

def cell_speed(state):
    depth = state[0]
    return jnp.maximum(jnp.abs(state[1] / depth), jnp.abs(state[2] / depth)) + jnp.sqrt(depth)

def fill_ghosts(near, coarse, own_near, relation, face_half):
    cells = near.shape[-1]
    middle = cells // 2
    same_level = near[:, :, 0]
    column = near[:, :, 0, :, 0, :]
    padded = jnp.concatenate([column[..., :1], column, column[..., -1:]], axis=-1)
    slope = padded[..., 2:] - padded[..., :-2]
    upper_half = (face_half == 1)[:, :, None, None]
    base_value = jnp.where(upper_half, column[..., middle:], column[..., :middle])
    base_slope = jnp.where(upper_half, slope[..., middle:], slope[..., :middle])
    base_value = jnp.repeat(base_value, 2, axis=-1)
    base_slope = jnp.repeat(base_slope, 2, axis=-1)
    weights = jnp.where(jnp.arange(cells) % 2 == 1, 0.125, -0.125).astype(near.dtype)
    interpolated = base_value + weights * base_slope
    coarser = jnp.broadcast_to(interpolated[:, :, :, None, :], same_level.shape)
    finer_ghost = jnp.concatenate([coarse[:, :, 0], coarse[:, :, 1]], axis=-1)
    mirror_sign = jnp.array([[1.0, -1.0, 1.0, 1.0], [1.0, -1.0, 1.0, 1.0], [1.0, 1.0, -1.0, 1.0], [1.0, 1.0, -1.0, 1.0]], near.dtype)
    mirror = own_near * mirror_sign[None, :, :, None, None]
    choose = relation[:, :, None, None, None]
    return jnp.where(choose == 0, mirror, jnp.where(choose == 1, same_level, jnp.where(choose == 2, coarser, finer_ghost)))

def physical(state, normal):
    depth = state[0]
    velocity = state[normal] / depth
    components = [state[normal], state[1] * velocity, state[2] * velocity, state[3] * velocity]
    components[normal] = components[normal] + 0.5 * depth * depth
    return (jnp.stack(components), jnp.abs(velocity) + jnp.sqrt(depth))

def flux_change(padded, normal):
    centre = padded[:, 1:-1]
    slope = 0.5 * (padded[:, 2:] - padded[:, :-2])
    left_state = (centre + 0.5 * slope)[:, :-1]
    right_state = (centre - 0.5 * slope)[:, 1:]
    left_flux, left_speed = physical(left_state, normal)
    right_flux, right_speed = physical(right_state, normal)
    widest = jnp.maximum(left_speed, right_speed)
    numeric_flux = 0.5 * (left_flux + right_flux) - 0.5 * widest * (right_state - left_state)
    return numeric_flux[:, 1:] - numeric_flux[:, :-1]

def advance(state, ghosts, step_ratio):
    sides = jnp.transpose(ghosts, (1, 2, 3, 4, 0))
    along_x = jnp.concatenate([sides[0][:, ::-1], state, sides[1]], axis=1)
    along_y = jnp.concatenate([sides[2][:, ::-1], jnp.swapaxes(state, 1, 2), sides[3]], axis=1)
    change = flux_change(along_x, 1) + jnp.swapaxes(flux_change(along_y, 2), 1, 2)
    return state - step_ratio * change

def reference(fields, patch_level, relation, face_half, neighbour, send_list):
    nfields = fields.shape[0]
    cells = fields.shape[1]
    spacing = jnp.exp2(finest_level - patch_level.astype(jnp.float32))
    top_speed = lax.optimization_barrier(jnp.max(cell_speed(fields), axis=(0, 1)))
    time_step = courant * jnp.min(spacing / top_speed)
    step_ratio = time_step / spacing
    packs = face_strips(fields).reshape(PATCHES, -1)
    offsets = jnp.array(list(range(1, HOPS + 1)) + [-(value + 1) for value in range(HOPS)], jnp.int32)
    opposite = jnp.array([1, 0, 3, 2], jnp.int32)[None, :, None]

    def one_device(device):
        start = (device * P_DEV).astype(jnp.int32)
        state = lax.dynamic_slice_in_dim(fields, start, P_DEV, 3)
        own_pack = lax.dynamic_slice_in_dim(packs, start, P_DEV, 0)
        source = jnp.clip(device - offsets, 0, N_PATCH - 1).astype(jnp.int32)
        chosen = send_list[source, jnp.arange(NOFF, dtype=jnp.int32)]
        rows = (source[:, None] * P_DEV + chosen).reshape(-1).astype(jnp.int32)
        ghost_pool = jnp.concatenate([own_pack, packs[rows]], axis=0)
        refs = lax.dynamic_slice_in_dim(neighbour, start, P_DEV, 0)
        kinds = lax.dynamic_slice_in_dim(relation, start, P_DEV, 0)
        halves = lax.dynamic_slice_in_dim(face_half, start, P_DEV, 0)
        picked = ghost_pool.reshape(POOL, 4, -1)[refs, opposite]
        whole = picked.reshape(P_DEV, 4, 2, nfields, 4, cells)
        ghosts = fill_ghosts(whole[..., 0:2, :], restrict(whole), face_strips(state)[..., 0:2, :], kinds, halves)
        return advance(state, ghosts, lax.dynamic_slice_in_dim(step_ratio, start, P_DEV, 0))
    stacked = lax.map(one_device, jnp.arange(N_PATCH, dtype=jnp.int32))
    advanced = jnp.transpose(stacked, (1, 2, 3, 0, 4)).reshape(nfields, cells, cells, PATCHES)
    return (advanced, time_step)
```

```python
import jax
import jax.numpy as jnp
from jax import lax
from jax.experimental import pallas as pl
from jax.experimental.pallas import tpu as pltpu
from jax.sharding import PartitionSpec as P

MESH = pl.DeviceIdType.MESH
CELLS = 32
NF = 4
LANES = 128
HOPS = 8
SEND = 8
PLANES = CELLS + 4
ROWS = 80
HALF = 8 * ROWS
DIM_Y, DIM_X, DIM_Z = 4, 4, 16
NEAR_Z = 4
COURANT = 0.4
F32 = jnp.float32


def offsets():
    return [k + 1 for k in range(HOPS)] + [-(k + 1) for k in range(HOPS)]


def wave(depth):
    r = lax.rsqrt(depth)
    return r * r, depth * r


def physical(state, normal):
    inverse, root = wave(state[0])
    momentum = state[normal]
    velocity = momentum * inverse
    flux = [momentum, state[1] * velocity, state[2] * velocity, state[3] * velocity]
    flux[normal] = flux[normal] + 0.5 * (state[0] * state[0])
    return flux, jnp.abs(velocity) + root


def cell_sides(load, j):
    uppers, lowers = [], []
    for c in range(NF):
        here = load(c, j)
        delta = 0.25 * (load(c, j + 1) - load(c, j - 1))
        uppers.append(here + delta)
        lowers.append(here - delta)
    return uppers, lowers


def interface(left, left_flux, left_speed, right, right_flux, right_speed):
    widest = jnp.maximum(left_speed, right_speed)
    return [(left_flux[c] + right_flux[c]) - widest * (right[c] - left[c]) for c in range(NF)]


def body(fields, level, relation, half, near, sends, out, step_out,
         px, py, cx, cy, level_v, relation_v, half_v, near_v, sends_v,
         own, own0, far, far0, send0, send1, recv0, recv1, edge, coarse, low,
         low_x, low_y, low_c, low_a, low_b, got_a,
         load_sem, small_sem, bulk_send, bulk_recv, low_send, low_recv):
    me = lax.axis_index("patch")
    core = lax.rem(me, 2)
    z = lax.rem(me // 2, DIM_Z)
    x = lax.rem(me // (2 * DIM_Z), DIM_X)
    y = me // (2 * DIM_Z * DIM_X)
    total = DIM_Y * DIM_X * DIM_Z * 2

    def place(yy, xx, zz, cc):
        return ((yy * DIM_X + xx) * DIM_Z + zz) * 2 + cc

    curve = [lax.rem(me + o + total, total) for o in offsets()]
    along_x = [place(y, lax.rem(x + k, DIM_X), z, core) for k in range(1, DIM_X)]
    along_y = [place(lax.rem(y + k, DIM_Y), x, z, core) for k in range(1, DIM_Y)]
    other = [place(y, x, z, 1 - core)]
    steps_z = [k for k in range(-NEAR_Z, NEAR_Z + 1) if k]
    along_z = [place(y, x, lax.rem(z + k + DIM_Z, DIM_Z), core) for k in steps_z]
    ends_z = [along_z[0], along_z[-1]]

    barrier = pltpu.get_barrier_semaphore()
    partners = curve + along_x + along_y + other + along_z
    for partner in partners:
        pl.semaphore_signal(barrier, inc=1, device_id=(partner,), device_id_type=MESH)

    loads = [pltpu.make_async_copy(fields.at[c], px.at[c, pl.ds(2, CELLS)], load_sem.at[c]) for c in range(NF)]
    smalls = [
        pltpu.make_async_copy(source, target, small_sem.at[n])
        for n, (source, target) in enumerate(
            [(level, level_v), (relation, relation_v), (half, half_v), (near, near_v), (sends, sends_v)]
        )
    ]
    for copy in loads + smalls:
        copy.start()
    for copy in loads + smalls:
        copy.wait()

    px2 = px.reshape(NF * PLANES * CELLS, LANES)
    py2 = py.reshape(NF * PLANES * CELLS, LANES)
    cy2 = cy.reshape(NF * CELLS * CELLS, LANES)
    out2 = out.reshape(NF * CELLS * CELLS, LANES)

    def scan_plane(i, best):
        state = [px[c, i + 2] for c in range(NF)]
        for c in range(NF):
            py2[pl.ds((c * PLANES + 2) * CELLS + i, CELLS, stride=CELLS), :] = state[c]
        inverse, root = wave(state[0])
        return jnp.maximum(best, jnp.maximum(jnp.abs(state[1]), jnp.abs(state[2])) * inverse + root)

    best = lax.fori_loop(0, CELLS, scan_plane, jnp.zeros((CELLS, LANES), F32), unroll=4)
    top_speed = jnp.max(best, axis=0, keepdims=True)
    spacing = lax.shift_left(jnp.ones((1, LANES), jnp.int32), 6 - level_v[...]).astype(F32)
    low[...] = spacing / top_speed

    def restricted(ref, first, second):
        evens = ref[pl.ds(first, 16, stride=2), :] + ref[pl.ds(second, 16, stride=2), :]
        odds = ref[pl.ds(first + 1, 16, stride=2), :] + ref[pl.ds(second + 1, 16, stride=2), :]
        return 0.25 * (evens + odds)

    for face in range(4):
        planes = px2 if face < 2 else py2
        for c in range(NF):
            at = [(c * PLANES + (2 + k if face % 2 == 0 else 33 - k)) * CELLS for k in range(4)]
            row = (face * NF + c) * ROWS
            own[pl.ds(row, CELLS), :] = planes[pl.ds(at[0], CELLS), :]
            own[pl.ds(row + 32, CELLS), :] = planes[pl.ds(at[1], CELLS), :]
            own[pl.ds(row + 64, 16), :] = restricted(planes, at[2], at[3])
            own0[pl.ds((face * NF + c) * 16, 16), :] = restricted(planes, at[0], at[1])

    lane = lax.broadcasted_iota(jnp.int32, (SEND, LANES), 1)
    slot = lax.broadcasted_iota(jnp.int32, (SEND, LANES), 0)
    listed = jnp.take_along_axis(sends_v[...], lane // SEND, axis=1)
    listed = jnp.sum(jnp.where(lax.rem(lane, SEND) == slot, listed, 0), axis=0, keepdims=True)
    listed = jnp.broadcast_to(listed, (LANES, LANES))
    for block in range(10):
        picked = jnp.take_along_axis(own[pl.ds(block * LANES, LANES), :], listed, axis=1)
        target = send0 if block < 5 else send1
        target[:, pl.ds(block % 5 * LANES, LANES)] = picked.T

    pl.semaphore_wait(barrier, len(partners))

    def tell(value, targets, slots, stage):
        for n, target in enumerate(targets):
            pltpu.make_async_remote_copy(
                src_ref=value, dst_ref=slots.at[n], send_sem=low_send.at[stage], recv_sem=low_recv.at[stage],
                device_id=(target,), device_id_type=MESH,
            ).start()

    def hear(slots, stage):
        pltpu.make_async_copy(slots, slots, low_recv.at[stage]).wait()
        return jnp.min(slots[...], axis=0)

    def exchange(source, target, part, which):
        for k in which:
            rows = pl.ds(k * SEND, SEND)
            pltpu.make_async_remote_copy(
                src_ref=source.at[rows], dst_ref=target.at[rows], send_sem=bulk_send.at[part],
                recv_sem=bulk_recv.at[part], device_id=(curve[k],), device_id_type=MESH,
            ).start()

    far_first = [7, 15, 6, 14, 5, 13, 4, 12, 3, 11, 2, 10, 1, 9, 0, 8]
    tell(low, along_z, low_a, 0)
    exchange(send0, recv0, 0, far_first)

    def interior(ref, normal, change):
        def row_tile(t, carry):
            rows = pl.ds(pl.multiple_of(t * 8, 8), 8)

            def load(c, j):
                return ref[c, j, rows, :]

            def advance(j, carried):
                left, left_flux, left_speed, before = carried
                upper, right = cell_sides(load, j + 1)
                right_flux, right_speed = physical(right, normal)
                flux = interface(left, left_flux, left_speed, right, right_flux, right_speed)
                for c in range(NF):
                    change[c, j - 2, rows, :] = flux[c] - before[c]
                upper_flux, upper_speed = physical(upper, normal)
                return upper, upper_flux, upper_speed, flux

            first, _ = cell_sides(load, 3)
            first_flux, first_speed = physical(first, normal)
            zero = jnp.zeros((8, LANES), F32)
            carried = advance(3, (first, first_flux, first_speed, [zero] * NF))
            last = lax.fori_loop(4, 32, advance, carried, unroll=4)
            for c in range(NF):
                change[c, 0, rows, :] = zero
                change[c, 30, rows, :] = -last[3][c]
                change[c, 31, rows, :] = zero
            return carry

        lax.fori_loop(0, 4, row_tile, 0)

    interior(px, 1, cx)

    lowest = jnp.minimum(low[...], hear(low_a, 0))
    got_a[...] = lowest
    tell(got_a, ends_z, low_b, 1)
    exchange(send1, recv1, 1, far_first)

    interior(py, 2, cy)

    lowest = jnp.minimum(lowest, hear(low_b, 1))
    low_x[0] = lowest
    tell(low_x.at[0], along_x, low_x.at[pl.ds(1, 3)], 2)
    lowest = jnp.minimum(lowest, hear(low_x.at[pl.ds(1, 3)], 2))
    low_y[0] = lowest
    tell(low_y.at[0], along_y, low_y.at[pl.ds(1, 3)], 3)
    lowest = jnp.minimum(lowest, hear(low_y.at[pl.ds(1, 3)], 3))
    low_c[0] = lowest
    tell(low_c.at[0], other, low_c.at[pl.ds(1, 1)], 4)
    lowest = jnp.minimum(lowest, hear(low_c.at[pl.ds(1, 1)], 4))
    time_step = COURANT * jnp.min(lowest, axis=1, keepdims=True)
    step_out[...] = jnp.broadcast_to(time_step, (1, LANES))
    ratio = jnp.broadcast_to(0.5 * (time_step / spacing), (CELLS, LANES))

    def settle(i, carry):
        for c in range(NF):
            turned = cy2[pl.ds(c * CELLS * CELLS + i, CELLS, stride=CELLS), :]
            out[c, i] = px[c, i + 2] - ratio * (cx[c, i] + turned)
        return carry

    lax.fori_loop(0, CELLS, settle, 0, unroll=2)

    def unpack(part):
        target = recv0 if part == 0 else recv1
        pltpu.make_async_copy(target, target, bulk_recv.at[part]).wait()
        for block in range(5):
            far[pl.ds((part * 5 + block) * LANES, LANES), :] = target[:, pl.ds(block * LANES, LANES)].T
        for face in (2 * part, 2 * part + 1):
            for c in range(NF):
                row = (face * NF + c) * ROWS
                far0[pl.ds((face * NF + c) * 16, 16), :] = restricted(far, row, row + 32)

    def pick(mine, theirs, row, count, index):
        spot = jnp.broadcast_to(lax.rem(index, LANES), (count, LANES))
        remote = jnp.broadcast_to(index, (count, LANES)) >= LANES
        return jnp.where(
            remote,
            jnp.take_along_axis(theirs[pl.ds(row, count), :], spot, axis=1),
            jnp.take_along_axis(mine[pl.ds(row, count), :], spot, axis=1),
        )

    def ghosts(face):
        planes = px if face < 2 else py
        opposite = face ^ 1
        kind = jnp.broadcast_to(relation_v[pl.ds(face, 1), :], (CELLS, LANES))
        upper = jnp.broadcast_to(half_v[pl.ds(face, 1), :], (16, LANES)) == 1
        first = near_v[face, pl.ds(0, 1), :]
        second = near_v[face, pl.ds(1, 1), :]
        for c in range(NF):
            row = (opposite * NF + c) * ROWS
            row0 = (opposite * NF + c) * 16
            level_same = [pick(own, far, row + 32 * g, CELLS, first) for g in range(2)]
            finer = [
                jnp.concatenate([pick(own0, far0, row0, 16, first), pick(own0, far0, row0, 16, second)], axis=0),
                jnp.concatenate([pick(own, far, row + 64, 16, first), pick(own, far, row + 64, 16, second)], axis=0),
            ]
            value = level_same[0]
            edge[pl.ds(8, CELLS), :] = value
            edge[pl.ds(7, 1), :] = value[0:1]
            edge[pl.ds(40, 1), :] = value[31:32]
            slope = edge[pl.ds(9, CELLS), :] - edge[pl.ds(7, CELLS), :]
            base = jnp.where(upper, value[16:], value[:16])
            lean = 0.125 * jnp.where(upper, slope[16:], slope[:16])
            coarse[pl.ds(0, 16, stride=2), :] = base - lean
            coarse[pl.ds(1, 16, stride=2), :] = base + lean
            wide = coarse[...]
            sign = -1.0 if c == 1 + face // 2 else 1.0
            for g in range(2):
                mirror = sign * own[pl.ds((face * NF + c) * ROWS + 32 * g, CELLS), :]
                ghost = jnp.where(
                    kind == 0,
                    mirror,
                    jnp.where(kind == 1, level_same[g], jnp.where(kind == 2, wide, finer[g])),
                )
                planes[c, 1 - g if face % 2 == 0 else 34 + g] = ghost

    def rim(ref, normal, apply):
        def load(c, j):
            return ref[c, j]

        for start, cells in ((1, ((0, -1, 0), (1, 1, None))), (32, ((30, None, 0), (31, 0, 1)))):
            sides = [cell_sides(load, j) for j in (start, start + 1, start + 2)]
            flux = []
            for n in range(2):
                left, right = sides[n][0], sides[n + 1][1]
                left_flux, left_speed = physical(left, normal)
                right_flux, right_speed = physical(right, normal)
                flux.append(interface(left, left_flux, left_speed, right, right_flux, right_speed))
            for c in range(NF):
                if start == 1:
                    apply(c, 0, flux[1][c] - flux[0][c])
                    apply(c, 1, -flux[1][c])
                else:
                    apply(c, 30, flux[0][c])
                    apply(c, 31, flux[1][c] - flux[0][c])

    def apply_x(c, i, change):
        out[c, i] = out[c, i] - ratio * change

    def apply_y(c, j, change):
        rows = pl.ds(c * CELLS * CELLS + j, CELLS, stride=CELLS)
        out2[rows, :] = out2[rows, :] - ratio * change

    unpack(0)
    ghosts(0)
    ghosts(1)
    rim(px, 1, apply_x)
    unpack(1)
    ghosts(2)
    ghosts(3)
    rim(py, 2, apply_y)

    for part, source in enumerate((send0, send1)):
        pltpu.make_async_copy(source, source, bulk_send.at[part]).wait()
    for stage, slots in enumerate((low_a, low_b, low_x.at[pl.ds(1, 3)], low_y.at[pl.ds(1, 3)], low_c.at[pl.ds(1, 1)])):
        pltpu.make_async_copy(slots, slots, low_send.at[stage]).wait()


def on_device(fields, patch_level, relation, face_half, neighbour, send_list):
    any_space = pl.BlockSpec(memory_space=pl.ANY)
    vmem = pl.BlockSpec(memory_space=pltpu.VMEM)
    cube = (NF, CELLS, CELLS, LANES)
    advanced, step = pl.pallas_call(
        body,
        out_shape=(jax.ShapeDtypeStruct(cube, F32), jax.ShapeDtypeStruct((1, LANES), F32)),
        in_specs=[any_space] * 6,
        out_specs=(vmem, vmem),
        scratch_shapes=[
            pltpu.VMEM((NF, PLANES, CELLS, LANES), F32),
            pltpu.VMEM((NF, PLANES, CELLS, LANES), F32),
            pltpu.VMEM(cube, F32),
            pltpu.VMEM(cube, F32),
            pltpu.VMEM((1, LANES), jnp.int32),
            pltpu.VMEM((4, LANES), jnp.int32),
            pltpu.VMEM((4, LANES), jnp.int32),
            pltpu.VMEM((4, 2, LANES), jnp.int32),
            pltpu.VMEM((SEND, LANES), jnp.int32),
            pltpu.VMEM((16 * ROWS, LANES), F32),
            pltpu.VMEM((256, LANES), F32),
            pltpu.VMEM((16 * ROWS, LANES), F32),
            pltpu.VMEM((256, LANES), F32),
            pltpu.VMEM((LANES, HALF), F32),
            pltpu.VMEM((LANES, HALF), F32),
            pltpu.VMEM((LANES, HALF), F32),
            pltpu.VMEM((LANES, HALF), F32),
            pltpu.VMEM((48, LANES), F32),
            pltpu.VMEM((CELLS, LANES), F32),
            pltpu.VMEM((1, LANES), F32),
            pltpu.VMEM((DIM_X, 1, LANES), F32),
            pltpu.VMEM((DIM_Y, 1, LANES), F32),
            pltpu.VMEM((2, 1, LANES), F32),
            pltpu.VMEM((2 * NEAR_Z, 1, LANES), F32),
            pltpu.VMEM((2, 1, LANES), F32),
            pltpu.VMEM((1, LANES), F32),
            pltpu.SemaphoreType.DMA((NF,)),
            pltpu.SemaphoreType.DMA((5,)),
            pltpu.SemaphoreType.DMA((2,)),
            pltpu.SemaphoreType.DMA((2,)),
            pltpu.SemaphoreType.DMA((5,)),
            pltpu.SemaphoreType.DMA((5,)),
        ],
        compiler_params=pltpu.CompilerParams(collective_id=0, has_side_effects=True),
    )(
        fields,
        patch_level.reshape(1, LANES),
        relation.T,
        face_half.T,
        jnp.transpose(neighbour, (1, 2, 0)),
        jnp.pad(send_list[0].T, ((0, 0), (0, LANES - NSLOT))),
    )
    return advanced, step[0, 0]


NSLOT = 2 * HOPS


def solution(mesh):
    return jax.shard_map(
        on_device,
        mesh=mesh,
        in_specs=(
            P(None, None, None, "patch"),
            P("patch"),
            P("patch", None),
            P("patch", None),
            P("patch", None, None),
            P("patch", None, None),
        ),
        out_specs=(P(None, None, None, "patch"), P()),
        check_vma=False,
    )
```

```python
import jax
import jax.numpy as jnp
from jax import lax
from jax.experimental import pallas as pl
from jax.experimental.pallas import tpu as pltpu
from jax.sharding import PartitionSpec as P

MESH = pl.DeviceIdType.MESH
CELLS = 32
NF = 4
LANES = 128
HOPS = 8
SEND = 8
PLANES = CELLS + 4
ROWS = 80
NSLOT = 2 * HOPS
PARTS = ((0, 3), (3, 2), (5, 3), (8, 2))
FAR_FIRST = [7, 15, 6, 14, 5, 13, 4, 12, 3, 11, 2, 10, 1, 9, 0, 8]
DIM_Y, DIM_X, DIM_Z = 4, 4, 16
NEAR_Z = 4
COURANT = 0.4
F32 = jnp.float32


def offsets():
    return [k + 1 for k in range(HOPS)] + [-(k + 1) for k in range(HOPS)]


def wave(depth):
    r = lax.rsqrt(depth)
    return r * r, depth * r


def physical(state, normal):
    inverse, root = wave(state[0])
    momentum = state[normal]
    velocity = momentum * inverse
    flux = [momentum, state[1] * velocity, state[2] * velocity, state[3] * velocity]
    flux[normal] = flux[normal] + 0.5 * (state[0] * state[0])
    return flux, jnp.abs(velocity) + root


def cell_sides(load, j):
    uppers, lowers = [], []
    for c in range(NF):
        here = load(c, j)
        delta = 0.25 * (load(c, j + 1) - load(c, j - 1))
        uppers.append(here + delta)
        lowers.append(here - delta)
    return uppers, lowers


def interface(left, left_flux, left_speed, right, right_flux, right_speed):
    widest = jnp.maximum(left_speed, right_speed)
    return [(left_flux[c] + right_flux[c]) - widest * (right[c] - left[c]) for c in range(NF)]


def body(fields, level, relation, half, near, sends, out, step_out,
         px, py, cx, cy, level_v, relation_v, half_v, near_v, sends_v,
         own, own0, far, far0, send, recv, edge, coarse, low, heard_z, heard_ends, heard_plane,
         edge_sem, load_sem, small_sem, bulk_send, bulk_recv, low_send, low_recv):
    me = lax.axis_index("patch")
    core = lax.rem(me, 2)
    z = lax.rem(me // 2, DIM_Z)
    x = lax.rem(me // (2 * DIM_Z), DIM_X)
    y = me // (2 * DIM_Z * DIM_X)
    total = DIM_Y * DIM_X * DIM_Z * 2

    def place(yy, xx, zz, cc):
        return ((yy * DIM_X + xx) * DIM_Z + zz) * 2 + cc

    def within(device):
        return jnp.logical_and(device >= 0, device < total)

    curve = [me + o for o in offsets()]
    sources = [me - o for o in offsets()]
    plane = [
        place(lax.rem(y + j, DIM_Y), lax.rem(x + k, DIM_X), z, cc)
        for j in range(DIM_Y) for k in range(DIM_X) for cc in (core, 1 - core)
    ][1:]
    steps_z = [k for k in range(-NEAR_Z, NEAR_Z + 1) if k]
    along_z = [place(y, x, lax.rem(z + k + DIM_Z, DIM_Z), core) for k in steps_z]
    ends_z = [along_z[0], along_z[-1]]

    barrier = pltpu.get_barrier_semaphore()
    expected = len(plane) + len(along_z)
    for partner in curve:
        expected = expected + within(partner).astype(jnp.int32)

        @pl.when(within(partner))
        def _():
            pl.semaphore_signal(barrier, inc=1, device_id=(partner,), device_id_type=MESH)

    for partner in along_z + plane:
        pl.semaphore_signal(barrier, inc=1, device_id=(partner,), device_id_type=MESH)

    smalls = [
        pltpu.make_async_copy(source, target, small_sem.at[n])
        for n, (source, target) in enumerate(
            [(sends, sends_v), (level, level_v), (relation, relation_v), (half, half_v), (near, near_v)]
        )
    ]
    edges = [
        pltpu.make_async_copy(
            fields.at[c, pl.ds(first, 4)], px.at[c, pl.ds(first + 2, 4)], edge_sem.at[2 * c + first // 28]
        )
        for c in range(NF) for first in (0, CELLS - 4)
    ]
    middles = [
        pltpu.make_async_copy(
            fields.at[c, pl.ds(4, CELLS - 8)], px.at[c, pl.ds(6, CELLS - 8)], load_sem.at[c]
        )
        for c in range(NF)
    ]
    for copy in smalls + edges + middles:
        copy.start()

    px2 = px.reshape(NF * PLANES * CELLS, LANES)
    py2 = py.reshape(NF * PLANES * CELLS, LANES)
    cy2 = cy.reshape(NF * CELLS * CELLS, LANES)
    out2 = out.reshape(NF * CELLS * CELLS, LANES)

    def restricted(ref, first, second):
        evens = ref[pl.ds(first, 16, stride=2), :] + ref[pl.ds(second, 16, stride=2), :]
        odds = ref[pl.ds(first + 1, 16, stride=2), :] + ref[pl.ds(second + 1, 16, stride=2), :]
        return 0.25 * (evens + odds)

    def pack(faces):
        for face in faces:
            planes = px2 if face < 2 else py2
            for c in range(NF):
                at = [(c * PLANES + (2 + k if face % 2 == 0 else 33 - k)) * CELLS for k in range(4)]
                row = (face * NF + c) * ROWS
                own[pl.ds(row, CELLS), :] = planes[pl.ds(at[0], CELLS), :]
                own[pl.ds(row + 32, CELLS), :] = planes[pl.ds(at[1], CELLS), :]
                own[pl.ds(row + 64, 16), :] = restricted(planes, at[2], at[3])
                own0[pl.ds((face * NF + c) * 16, 16), :] = restricted(planes, at[0], at[1])

    for copy in smalls + edges:
        copy.wait()
    pack((0, 1))

    lane = lax.broadcasted_iota(jnp.int32, (SEND, LANES), 1)
    slot = lax.broadcasted_iota(jnp.int32, (SEND, LANES), 0)
    listed = jnp.take_along_axis(jnp.concatenate([sends_v[...], jnp.zeros((SEND, LANES - NSLOT), jnp.int32)], axis=1), lane // SEND, axis=1)
    listed = jnp.sum(jnp.where(lax.rem(lane, SEND) == slot, listed, 0), axis=0, keepdims=True)
    listed = jnp.broadcast_to(listed, (LANES, LANES))
    def offer(tiles):
        for tile in tiles:
            columns = pl.ds(tile * LANES, LANES)
            send[:, columns] = jnp.take_along_axis(own[columns, :], listed, axis=1).T

    offer(range(5))
    for copy in middles:
        copy.wait()

    def scan_plane(i, best):
        state = [px[c, i + 2] for c in range(NF)]
        for c in range(NF):
            py2[pl.ds((c * PLANES + 2) * CELLS + i, CELLS, stride=CELLS), :] = state[c]
        inverse, root = wave(state[0])
        return jnp.maximum(best, jnp.maximum(jnp.abs(state[1]), jnp.abs(state[2])) * inverse + root)

    best = lax.fori_loop(0, CELLS, scan_plane, jnp.zeros((CELLS, LANES), F32), unroll=4)
    top_speed = jnp.max(best, axis=0, keepdims=True)
    spacing = lax.shift_left(jnp.ones((1, LANES), jnp.int32), 6 - level_v[...]).astype(F32)
    low[0] = spacing / top_speed

    def tell(value, targets, slots, stage):
        for n, target in enumerate(targets):
            pltpu.make_async_remote_copy(
                src_ref=value, dst_ref=slots.at[n], send_sem=low_send.at[stage], recv_sem=low_recv.at[stage],
                device_id=(target,), device_id_type=MESH,
            ).start()

    def hear(slots, stage):
        pltpu.make_async_copy(slots, slots, low_recv.at[stage]).wait()
        return jnp.min(slots[...], axis=0)

    def block_at(ref, part, k):
        return ref.at[pl.ds(k * SEND, SEND), pl.ds(PARTS[part][0] * LANES, PARTS[part][1] * LANES)]

    def exchange(part):
        for k in FAR_FIRST:

            @pl.when(within(curve[k]))
            def _():
                pltpu.make_async_remote_copy(
                    src_ref=block_at(send, part, k), dst_ref=block_at(recv, part, k), send_sem=bulk_send.at[k],
                    recv_sem=bulk_recv.at[part, k], device_id=(curve[k],), device_id_type=MESH,
                ).start()

    def arrived(part):
        for k in range(NSLOT):

            @pl.when(within(sources[k]))
            def _():
                block = block_at(recv, part, k)
                pltpu.make_async_copy(block, block, bulk_recv.at[part, k]).wait()

        first, count = PARTS[part]
        for tile in range(first, first + count):
            columns = pl.ds(tile * LANES, LANES)
            far[columns, :] = recv[:, columns].T

    pl.semaphore_wait(barrier, expected)
    tell(low.at[0], along_z, heard_z, 0)
    exchange(0)

    pack((2, 3))
    offer(range(5, 10))

    def interior(ref, normal, change):
        def row_tile(t, carry):
            rows = pl.ds(pl.multiple_of(t * 8, 8), 8)

            def load(c, j):
                return ref[c, j, rows, :]

            def advance(j, carried):
                left, left_flux, left_speed, before = carried
                upper, right = cell_sides(load, j + 1)
                right_flux, right_speed = physical(right, normal)
                flux = interface(left, left_flux, left_speed, right, right_flux, right_speed)
                for c in range(NF):
                    change[c, j - 2, rows, :] = flux[c] - before[c]
                upper_flux, upper_speed = physical(upper, normal)
                return upper, upper_flux, upper_speed, flux

            first, _ = cell_sides(load, 3)
            first_flux, first_speed = physical(first, normal)
            zero = jnp.zeros((8, LANES), F32)
            carried = advance(3, (first, first_flux, first_speed, [zero] * NF))
            last = lax.fori_loop(4, 32, advance, carried, unroll=4)
            for c in range(NF):
                change[c, 0, rows, :] = zero
                change[c, 30, rows, :] = -last[3][c]
                change[c, 31, rows, :] = zero
            return carry

        lax.fori_loop(0, 4, row_tile, 0)

    interior(px, 1, cx)

    low[1] = jnp.minimum(low[0], hear(heard_z, 0))
    tell(low.at[1], ends_z, heard_ends, 1)
    for part in (1, 2, 3):
        exchange(part)

    interior(py, 2, cy)

    low[2] = jnp.minimum(low[1], hear(heard_ends, 1))
    tell(low.at[2], plane, heard_plane, 2)

    def shallow(face):
        for c in range(NF):
            row = (face * NF + c) * ROWS
            far0[pl.ds((face * NF + c) * 16, 16), :] = restricted(far, row, row + 32)

    def pick(mine, theirs, row, count, index):
        spot = jnp.broadcast_to(lax.rem(index, LANES), (count, LANES))
        remote = jnp.broadcast_to(index, (count, LANES)) >= LANES
        return jnp.where(
            remote,
            jnp.take_along_axis(theirs[pl.ds(row, count), :], spot, axis=1),
            jnp.take_along_axis(mine[pl.ds(row, count), :], spot, axis=1),
        )

    def ghosts(face):
        planes = px if face < 2 else py
        opposite = face ^ 1
        kind = jnp.broadcast_to(relation_v[pl.ds(face, 1), :], (CELLS, LANES))
        upper = jnp.broadcast_to(half_v[pl.ds(face, 1), :], (16, LANES)) == 1
        first = near_v[face, pl.ds(0, 1), :]
        second = near_v[face, pl.ds(1, 1), :]
        for c in range(NF):
            row = (opposite * NF + c) * ROWS
            row0 = (opposite * NF + c) * 16
            level_same = [pick(own, far, row + 32 * g, CELLS, first) for g in range(2)]
            finer = [
                jnp.concatenate([pick(own0, far0, row0, 16, first), pick(own0, far0, row0, 16, second)], axis=0),
                jnp.concatenate([pick(own, far, row + 64, 16, first), pick(own, far, row + 64, 16, second)], axis=0),
            ]
            value = level_same[0]
            edge[pl.ds(8, CELLS), :] = value
            edge[pl.ds(7, 1), :] = value[0:1]
            edge[pl.ds(40, 1), :] = value[31:32]
            slope = edge[pl.ds(9, CELLS), :] - edge[pl.ds(7, CELLS), :]
            base = jnp.where(upper, value[16:], value[:16])
            lean = 0.125 * jnp.where(upper, slope[16:], slope[:16])
            coarse[pl.ds(0, 16, stride=2), :] = base - lean
            coarse[pl.ds(1, 16, stride=2), :] = base + lean
            wide = coarse[...]
            sign = -1.0 if c == 1 + face // 2 else 1.0
            for g in range(2):
                mirror = sign * own[pl.ds((face * NF + c) * ROWS + 32 * g, CELLS), :]
                ghost = jnp.where(
                    kind == 0,
                    mirror,
                    jnp.where(kind == 1, level_same[g], jnp.where(kind == 2, wide, finer[g])),
                )
                planes[c, 1 - g if face % 2 == 0 else 34 + g] = ghost

    def rim(ref, normal, face, apply):
        start = 1 if face % 2 == 0 else 32

        def load(c, j):
            return ref[c, j]

        sides = [cell_sides(load, j) for j in (start, start + 1, start + 2)]
        flux = []
        for n in range(2):
            left, right = sides[n][0], sides[n + 1][1]
            left_flux, left_speed = physical(left, normal)
            right_flux, right_speed = physical(right, normal)
            flux.append(interface(left, left_flux, left_speed, right, right_flux, right_speed))
        for c in range(NF):
            if face % 2 == 0:
                apply(c, 0, flux[1][c] - flux[0][c])
                apply(c, 1, -flux[1][c])
            else:
                apply(c, 30, flux[0][c])
                apply(c, 31, flux[1][c] - flux[0][c])

    def apply_x(c, i, change):
        cx[c, i] = cx[c, i] + change

    arrived(0)
    shallow(0)
    ghosts(1)
    rim(px, 1, 1, apply_x)
    arrived(1)
    shallow(1)
    ghosts(0)
    rim(px, 1, 0, apply_x)

    lowest = jnp.minimum(low[2], hear(heard_plane, 2))
    time_step = COURANT * jnp.min(lowest, axis=1, keepdims=True)
    step_out[...] = jnp.broadcast_to(time_step, (1, LANES))
    ratio = jnp.broadcast_to(0.5 * (time_step / spacing), (CELLS, LANES))

    def settle(i, carry):
        for c in range(NF):
            turned = cy2[pl.ds(c * CELLS * CELLS + i, CELLS, stride=CELLS), :]
            out[c, i] = px[c, i + 2] - ratio * (cx[c, i] + turned)
        return carry

    lax.fori_loop(0, CELLS, settle, 0, unroll=2)

    def apply_y(c, j, change):
        rows = pl.ds(c * CELLS * CELLS + j, CELLS, stride=CELLS)
        out2[rows, :] = out2[rows, :] - ratio * change

    for stage, slots in enumerate((heard_z, heard_ends, heard_plane)):
        pltpu.make_async_copy(slots, slots, low_send.at[stage]).wait()

    arrived(2)
    shallow(2)
    ghosts(3)
    rim(py, 2, 3, apply_y)
    arrived(3)
    shallow(3)
    ghosts(2)
    rim(py, 2, 2, apply_y)

    for k in range(NSLOT):

        @pl.when(within(curve[k]))
        def _():
            block = send.at[pl.ds(k * SEND, SEND)]
            pltpu.make_async_copy(block, block, bulk_send.at[k]).wait()


def on_device(fields, patch_level, relation, face_half, neighbour, send_list):
    any_space = pl.BlockSpec(memory_space=pl.ANY)
    vmem = pl.BlockSpec(memory_space=pltpu.VMEM)
    cube = (NF, CELLS, CELLS, LANES)
    advanced, step = pl.pallas_call(
        body,
        out_shape=(pltpu.VMEM(cube, F32), jax.ShapeDtypeStruct((1, LANES), F32)),
        in_specs=[any_space] * 6,
        out_specs=(vmem, vmem),
        scratch_shapes=[
            pltpu.VMEM((NF, PLANES, CELLS, LANES), F32),
            pltpu.VMEM((NF, PLANES, CELLS, LANES), F32),
            pltpu.VMEM(cube, F32),
            pltpu.VMEM(cube, F32),
            pltpu.VMEM((1, LANES), jnp.int32),
            pltpu.VMEM((4, LANES), jnp.int32),
            pltpu.VMEM((4, LANES), jnp.int32),
            pltpu.VMEM((4, 2, LANES), jnp.int32),
            pltpu.VMEM((SEND, NSLOT), jnp.int32),
            pltpu.VMEM((16 * ROWS, LANES), F32),
            pltpu.VMEM((256, LANES), F32),
            pltpu.VMEM((16 * ROWS, LANES), F32),
            pltpu.VMEM((256, LANES), F32),
            pltpu.VMEM((LANES, 16 * ROWS), F32),
            pltpu.VMEM((LANES, 16 * ROWS), F32),
            pltpu.VMEM((48, LANES), F32),
            pltpu.VMEM((CELLS, LANES), F32),
            pltpu.VMEM((3, 1, LANES), F32),
            pltpu.VMEM((2 * NEAR_Z, 1, LANES), F32),
            pltpu.VMEM((2, 1, LANES), F32),
            pltpu.VMEM((2 * DIM_X * DIM_Y - 1, 1, LANES), F32),
            pltpu.SemaphoreType.DMA((2 * NF,)),
            pltpu.SemaphoreType.DMA((NF,)),
            pltpu.SemaphoreType.DMA((5,)),
            pltpu.SemaphoreType.DMA((NSLOT,)),
            pltpu.SemaphoreType.DMA((len(PARTS), NSLOT)),
            pltpu.SemaphoreType.DMA((3,)),
            pltpu.SemaphoreType.DMA((3,)),
        ],
        compiler_params=pltpu.CompilerParams(collective_id=0, has_side_effects=True),
    )(
        fields,
        patch_level.reshape(1, LANES),
        relation.T,
        face_half.T,
        jnp.transpose(neighbour, (1, 2, 0)),
        send_list[0].T,
    )
    return advanced, step[0, 0]


def solution(mesh):
    return jax.shard_map(
        on_device,
        mesh=mesh,
        in_specs=(
            P(None, None, None, "patch"),
            P("patch"),
            P("patch", None),
            P("patch", None),
            P("patch", None, None),
            P("patch", None, None),
        ),
        out_specs=(P(None, None, None, "patch"), P()),
        check_vma=False,
    )
```

```python
import jax
import jax.numpy as jnp
from jax import lax
from jax.experimental import pallas as pl
from jax.experimental.pallas import tpu as pltpu
from jax.sharding import PartitionSpec as P

MESH = pl.DeviceIdType.MESH
CELLS = 32
NF = 4
LANES = 128
HOPS = 8
SEND = 8
PLANES = CELLS + 4
ROWS = 80
NSLOT = 2 * HOPS
PARTS = ((0, 3), (3, 2), (5, 2), (7, 2))
TILES = 9
REST = 32
FAR_FIRST = [7, 15, 6, 14, 5, 13, 4, 12, 3, 11, 2, 10, 1, 9, 0, 8]
DIM_Y, DIM_X, DIM_Z = 4, 4, 16
NEAR_Z = 4
COURANT = 0.4
F32 = jnp.float32


def offsets():
    return [k + 1 for k in range(HOPS)] + [-(k + 1) for k in range(HOPS)]


def wave(depth):
    r = lax.rsqrt(depth)
    return r * r, depth * r


def physical(state, normal):
    inverse, root = wave(state[0])
    momentum = state[normal]
    velocity = momentum * inverse
    flux = [momentum, state[1] * velocity, state[2] * velocity, state[3] * velocity]
    flux[normal] = flux[normal] + 0.5 * (state[0] * state[0])
    return flux, jnp.abs(velocity) + root


def cell_sides(load, j):
    uppers, lowers = [], []
    for c in range(NF):
        here = load(c, j)
        delta = 0.25 * (load(c, j + 1) - load(c, j - 1))
        uppers.append(here + delta)
        lowers.append(here - delta)
    return uppers, lowers


def interface(left, left_flux, left_speed, right, right_flux, right_speed):
    widest = jnp.maximum(left_speed, right_speed)
    return [(left_flux[c] + right_flux[c]) - widest * (right[c] - left[c]) for c in range(NF)]


def body(fields, level, relation, half, near, sends, out, step_out,
         px, py, cx, cy, level_v, relation_v, half_v, near_v, sends_v,
         own, own0, far, far0, lean, far_lean, spare, send, recv, rest_send, rest_recv, edge, coarse, low, heard_z, heard_ends, heard_plane,
         edge_sem, load_sem, small_sem, bulk_send, bulk_recv, rest_sem_send, rest_sem_recv, low_send, low_recv):
    me = lax.axis_index("patch")
    core = lax.rem(me, 2)
    z = lax.rem(me // 2, DIM_Z)
    x = lax.rem(me // (2 * DIM_Z), DIM_X)
    y = me // (2 * DIM_Z * DIM_X)
    total = DIM_Y * DIM_X * DIM_Z * 2

    def place(yy, xx, zz, cc):
        return ((yy * DIM_X + xx) * DIM_Z + zz) * 2 + cc

    def within(device):
        return jnp.logical_and(device >= 0, device < total)

    curve = [me + o for o in offsets()]
    sources = [me - o for o in offsets()]
    plane = [
        place(lax.rem(y + j, DIM_Y), lax.rem(x + k, DIM_X), z, cc)
        for j in range(DIM_Y) for k in range(DIM_X) for cc in (core, 1 - core)
    ][1:]
    steps_z = [k for k in range(-NEAR_Z, NEAR_Z + 1) if k]
    along_z = [place(y, x, lax.rem(z + k + DIM_Z, DIM_Z), core) for k in steps_z]
    ends_z = [along_z[0], along_z[-1]]

    barrier = pltpu.get_barrier_semaphore()
    expected = len(plane) + len(along_z)
    for partner in curve:
        expected = expected + within(partner).astype(jnp.int32)

        @pl.when(within(partner))
        def _():
            pl.semaphore_signal(barrier, inc=1, device_id=(partner,), device_id_type=MESH)

    for partner in along_z + plane:
        pl.semaphore_signal(barrier, inc=1, device_id=(partner,), device_id_type=MESH)

    smalls = [
        pltpu.make_async_copy(source, target, small_sem.at[n])
        for n, (source, target) in enumerate(
            [(sends, sends_v), (level, level_v), (relation, relation_v), (half, half_v), (near, near_v)]
        )
    ]
    edges = [
        pltpu.make_async_copy(
            fields.at[c, pl.ds(first, 4)], px.at[c, pl.ds(first + 2, 4)], edge_sem.at[2 * c + first // 28]
        )
        for c in range(NF) for first in (0, CELLS - 4)
    ]
    middles = [
        pltpu.make_async_copy(
            fields.at[c, pl.ds(4, CELLS - 8)], px.at[c, pl.ds(6, CELLS - 8)], load_sem.at[c]
        )
        for c in range(NF)
    ]
    for copy in smalls + edges + middles:
        copy.start()

    px2 = px.reshape(NF * PLANES * CELLS, LANES)
    py2 = py.reshape(NF * PLANES * CELLS, LANES)
    out2 = out.reshape(NF * CELLS * CELLS, LANES)

    def restricted(ref, first, second):
        evens = ref[pl.ds(first, 16, stride=2), :] + ref[pl.ds(second, 16, stride=2), :]
        odds = ref[pl.ds(first + 1, 16, stride=2), :] + ref[pl.ds(second + 1, 16, stride=2), :]
        return 0.25 * (evens + odds)

    def pack(faces):
        for face in faces:
            planes = px2 if face < 2 else py2
            for c in range(NF):
                at = [(c * PLANES + (2 + k if face % 2 == 0 else 33 - k)) * CELLS for k in range(4)]
                row = (face * NF + c) * ROWS
                own[pl.ds(row, CELLS), :] = planes[pl.ds(at[0], CELLS), :]
                own[pl.ds(row + 32, CELLS), :] = planes[pl.ds(at[1], CELLS), :]
                own[pl.ds(row + 64, 16), :] = restricted(planes, at[2], at[3])
                own0[pl.ds((face * NF + c) * 16, 16), :] = restricted(planes, at[0], at[1])

    for copy in smalls + edges:
        copy.wait()
    pack((0, 1))

    lane = lax.broadcasted_iota(jnp.int32, (SEND, LANES), 1)
    slot = lax.broadcasted_iota(jnp.int32, (SEND, LANES), 0)
    listed = jnp.take_along_axis(jnp.concatenate([sends_v[...], jnp.zeros((SEND, LANES - NSLOT), jnp.int32)], axis=1), lane // SEND, axis=1)
    listed = jnp.sum(jnp.where(lax.rem(lane, SEND) == slot, listed, 0), axis=0, keepdims=True)
    listed = jnp.broadcast_to(listed, (LANES, LANES))
    def offer(tiles):
        for tile in tiles:
            columns = pl.ds(tile * LANES, LANES)
            rows = own[columns, :] if tile < 5 else lean[pl.ds((tile - 5) * LANES, LANES), :]
            send[:, columns] = jnp.take_along_axis(rows, listed, axis=1).T

    def thin():
        for face in (2, 3):
            for c in range(NF):
                row = (face * NF + c) * ROWS
                for g in range(2):
                    lean[pl.ds((face - 2) * 256 + (2 * c + g) * 28, 28), :] = own[pl.ds(row + 32 * g + 2, 28), :]
                lean[pl.ds((face - 2) * 256 + 224 + 8 * c, 8), :] = own[pl.ds(row + 66, 8), :]
                lean[pl.ds(512 + (face - 2) * 16 + 4 * c, 4), :] = own[pl.ds(row + 74, 4), :]

    group = lax.broadcasted_iota(jnp.int32, (REST, LANES), 1) // REST

    def offer_rest():
        spare[...] = jnp.take_along_axis(lean[pl.ds(4 * LANES, LANES), :], listed, axis=1).T
        merged = spare[pl.ds(0, REST, stride=4), :]
        for j in range(1, 4):
            merged = jnp.where(group == j, pltpu.roll(spare[pl.ds(j, REST, stride=4), :], j * REST, 1), merged)
        rest_send[...] = merged

    offer(range(5))
    for copy in middles:
        copy.wait()

    def scan_block(n, best):
        low_x, low_y = pl.multiple_of(n // 4 * 8, 8), pl.multiple_of(lax.rem(n, 4) * 8, 8)
        state = [px[c, pl.ds(low_x + 2, 8), pl.ds(low_y, 8), :] for c in range(NF)]
        for c in range(NF):
            py[c, pl.ds(low_y + 2, 8), pl.ds(low_x, 8), :] = jnp.swapaxes(state[c], 0, 1)
        inverse, root = wave(state[0])
        return jnp.maximum(best, jnp.maximum(jnp.abs(state[1]), jnp.abs(state[2])) * inverse + root)

    best = lax.fori_loop(0, 16, scan_block, jnp.zeros((8, 8, LANES), F32))
    top_speed = jnp.max(jnp.max(best, axis=0), axis=0, keepdims=True)
    spacing = lax.shift_left(jnp.ones((1, LANES), jnp.int32), 6 - level_v[...]).astype(F32)
    low[0] = spacing / top_speed

    def tell(value, targets, slots, stage):
        for n, target in enumerate(targets):
            pltpu.make_async_remote_copy(
                src_ref=value, dst_ref=slots.at[n], send_sem=low_send.at[stage], recv_sem=low_recv.at[stage],
                device_id=(target,), device_id_type=MESH,
            ).start()

    def hear(slots, stage):
        pltpu.make_async_copy(slots, slots, low_recv.at[stage]).wait()
        return jnp.min(slots[...], axis=0)

    def block_at(ref, part, k):
        return ref.at[pl.ds(k * SEND, SEND), pl.ds(PARTS[part][0] * LANES, PARTS[part][1] * LANES)]

    def exchange(part):
        for k in FAR_FIRST:

            @pl.when(within(curve[k]))
            def _():
                pltpu.make_async_remote_copy(
                    src_ref=block_at(send, part, k), dst_ref=block_at(recv, part, k), send_sem=bulk_send.at[k],
                    recv_sem=bulk_recv.at[part, k], device_id=(curve[k],), device_id_type=MESH,
                ).start()
                if part == 2:
                    rows = pl.ds(2 * k, 2)
                    pltpu.make_async_remote_copy(
                        src_ref=rest_send.at[rows], dst_ref=rest_recv.at[rows], send_sem=rest_sem_send.at[k],
                        recv_sem=rest_sem_recv.at[k], device_id=(curve[k],), device_id_type=MESH,
                    ).start()

    def arrived(part):
        for k in range(NSLOT):

            @pl.when(within(sources[k]))
            def _():
                block = block_at(recv, part, k)
                pltpu.make_async_copy(block, block, bulk_recv.at[part, k]).wait()
                if part == 2:
                    block = rest_recv.at[pl.ds(2 * k, 2)]
                    pltpu.make_async_copy(block, block, rest_sem_recv.at[k]).wait()

        first, count = PARTS[part]
        for tile in range(first, first + count):
            columns = pl.ds(tile * LANES, LANES)
            if tile < 5:
                far[columns, :] = recv[:, columns].T
            else:
                far_lean[pl.ds((tile - 5) * LANES, LANES), :] = recv[:, columns].T
        if part == 2:
            for j in range(4):
                spare[pl.ds(j, REST, stride=4), :] = pltpu.roll(rest_recv[...], (LANES - j * REST) % LANES, 1)
            far_lean[pl.ds(4 * LANES, LANES), :] = spare[...].T

    pl.semaphore_wait(barrier, expected)
    tell(low.at[0], along_z, heard_z, 0)
    exchange(0)

    pack((2, 3))
    thin()
    offer(range(5, TILES))
    offer_rest()

    def interior(ref, normal, change):
        def row_tile(t, carry):
            rows = pl.ds(pl.multiple_of(t * 8, 8), 8)

            def load(c, j):
                return ref[c, j, rows, :]

            def advance(j, carried):
                left, left_flux, left_speed, before = carried
                upper, right = cell_sides(load, j + 1)
                right_flux, right_speed = physical(right, normal)
                flux = interface(left, left_flux, left_speed, right, right_flux, right_speed)
                for c in range(NF):
                    change[c, j - 2, rows, :] = flux[c] - before[c]
                upper_flux, upper_speed = physical(upper, normal)
                return upper, upper_flux, upper_speed, flux

            first, _ = cell_sides(load, 3)
            first_flux, first_speed = physical(first, normal)
            zero = jnp.zeros((8, LANES), F32)
            carried = advance(3, (first, first_flux, first_speed, [zero] * NF))
            last = lax.fori_loop(4, 32, advance, carried, unroll=4)
            for c in range(NF):
                change[c, 0, rows, :] = zero
                change[c, 30, rows, :] = -last[3][c]
                change[c, 31, rows, :] = zero
            return carry

        lax.fori_loop(0, 4, row_tile, 0)

    low[1] = jnp.minimum(low[0], hear(heard_z, 0))
    tell(low.at[1], ends_z, heard_ends, 1)
    for part in (1, 2, 3):
        exchange(part)

    interior(px, 1, cx)
    interior(py, 2, cy)

    low[2] = jnp.minimum(low[1], hear(heard_ends, 1))
    tell(low.at[2], plane, heard_plane, 2)

    def corners():
        for face in (2, 3):
            for c in range(NF):
                row = (face * NF + c) * ROWS
                west, east = c * ROWS, (NF + c) * ROWS
                west0, east0 = c * 16, (NF + c) * 16
                for g in range(2):
                    side = g if face == 2 else 31 - g
                    for t, source in ((0, west), (1, west + 32), (30, east + 32), (31, east)):
                        far[pl.ds(row + 32 * g + t, 1), :] = far[pl.ds(source + side, 1), :]
                side = 1 if face == 2 else 14
                far[pl.ds(row + 64, 1), :] = far0[pl.ds(west0 + side, 1), :]
                far[pl.ds(row + 65, 1), :] = far[pl.ds(west + 64 + side, 1), :]
                far[pl.ds(row + 78, 1), :] = far[pl.ds(east + 64 + side, 1), :]
                far[pl.ds(row + 79, 1), :] = far0[pl.ds(east0 + side, 1), :]

    def fatten(face):
        for c in range(NF):
            row = (face * NF + c) * ROWS
            for g in range(2):
                far[pl.ds(row + 32 * g + 2, 28), :] = far_lean[pl.ds((face - 2) * 256 + (2 * c + g) * 28, 28), :]
            far[pl.ds(row + 66, 8), :] = far_lean[pl.ds((face - 2) * 256 + 224 + 8 * c, 8), :]
            far[pl.ds(row + 74, 4), :] = far_lean[pl.ds(512 + (face - 2) * 16 + 4 * c, 4), :]

    def shallow(face):
        for c in range(NF):
            row = (face * NF + c) * ROWS
            far0[pl.ds((face * NF + c) * 16, 16), :] = restricted(far, row, row + 32)

    def pick(mine, theirs, row, count, index):
        spot = jnp.broadcast_to(lax.rem(index, LANES), (count, LANES))
        remote = jnp.broadcast_to(index, (count, LANES)) >= LANES
        return jnp.where(
            remote,
            jnp.take_along_axis(theirs[pl.ds(row, count), :], spot, axis=1),
            jnp.take_along_axis(mine[pl.ds(row, count), :], spot, axis=1),
        )

    def ghosts(face):
        planes = px if face < 2 else py
        opposite = face ^ 1
        kind = jnp.broadcast_to(relation_v[pl.ds(face, 1), :], (CELLS, LANES))
        upper = jnp.broadcast_to(half_v[pl.ds(face, 1), :], (16, LANES)) == 1
        first = near_v[face, pl.ds(0, 1), :]
        second = near_v[face, pl.ds(1, 1), :]
        for c in range(NF):
            row = (opposite * NF + c) * ROWS
            row0 = (opposite * NF + c) * 16
            level_same = [pick(own, far, row + 32 * g, CELLS, first) for g in range(2)]
            finer = [
                jnp.concatenate([pick(own0, far0, row0, 16, first), pick(own0, far0, row0, 16, second)], axis=0),
                jnp.concatenate([pick(own, far, row + 64, 16, first), pick(own, far, row + 64, 16, second)], axis=0),
            ]
            value = level_same[0]
            edge[pl.ds(8, CELLS), :] = value
            edge[pl.ds(7, 1), :] = value[0:1]
            edge[pl.ds(40, 1), :] = value[31:32]
            slope = edge[pl.ds(9, CELLS), :] - edge[pl.ds(7, CELLS), :]
            base = jnp.where(upper, value[16:], value[:16])
            lean = 0.125 * jnp.where(upper, slope[16:], slope[:16])
            coarse[pl.ds(0, 16, stride=2), :] = base - lean
            coarse[pl.ds(1, 16, stride=2), :] = base + lean
            wide = coarse[...]
            sign = -1.0 if c == 1 + face // 2 else 1.0
            for g in range(2):
                mirror = sign * own[pl.ds((face * NF + c) * ROWS + 32 * g, CELLS), :]
                ghost = jnp.where(
                    kind == 0,
                    mirror,
                    jnp.where(kind == 1, level_same[g], jnp.where(kind == 2, wide, finer[g])),
                )
                planes[c, 1 - g if face % 2 == 0 else 34 + g] = ghost

    def rim(ref, normal, face, apply):
        start = 1 if face % 2 == 0 else 32

        def load(c, j):
            return ref[c, j]

        sides = [cell_sides(load, j) for j in (start, start + 1, start + 2)]
        flux = []
        for n in range(2):
            left, right = sides[n][0], sides[n + 1][1]
            left_flux, left_speed = physical(left, normal)
            right_flux, right_speed = physical(right, normal)
            flux.append(interface(left, left_flux, left_speed, right, right_flux, right_speed))
        for c in range(NF):
            if face % 2 == 0:
                apply(c, 0, flux[1][c] - flux[0][c])
                apply(c, 1, -flux[1][c])
            else:
                apply(c, 30, flux[0][c])
                apply(c, 31, flux[1][c] - flux[0][c])

    def apply_x(c, i, change):
        cx[c, i] = cx[c, i] + change

    def join(n, carry):
        low_x, low_y = pl.multiple_of(n // 4 * 8, 8), pl.multiple_of(lax.rem(n, 4) * 8, 8)
        for c in range(NF):
            turned = jnp.swapaxes(cy[c, pl.ds(low_y, 8), pl.ds(low_x, 8), :], 0, 1)
            at = (c, pl.ds(low_x, 8), pl.ds(low_y, 8))
            cx[at] = cx[at] + turned
        return carry

    lax.fori_loop(0, 16, join, 0)

    arrived(0)
    shallow(0)
    ghosts(1)
    rim(px, 1, 1, apply_x)
    arrived(1)
    shallow(1)
    ghosts(0)
    rim(px, 1, 0, apply_x)
    corners()

    lowest = jnp.minimum(low[2], hear(heard_plane, 2))
    time_step = COURANT * jnp.min(lowest, axis=1, keepdims=True)
    step_out[...] = jnp.broadcast_to(time_step, (1, LANES))
    ratio = jnp.broadcast_to(0.5 * (time_step / spacing), (CELLS, LANES))

    def settle(i, carry):
        for c in range(NF):
            out[c, i] = px[c, i + 2] - ratio * cx[c, i]
        return carry

    lax.fori_loop(0, CELLS, settle, 0, unroll=2)

    def apply_y(c, j, change):
        rows = pl.ds(c * CELLS * CELLS + j, CELLS, stride=CELLS)
        out2[rows, :] = out2[rows, :] - ratio * change

    for stage, slots in enumerate((heard_z, heard_ends, heard_plane)):
        pltpu.make_async_copy(slots, slots, low_send.at[stage]).wait()

    arrived(2)
    fatten(2)
    shallow(2)
    ghosts(3)
    rim(py, 2, 3, apply_y)
    arrived(3)
    fatten(3)
    shallow(3)
    ghosts(2)
    rim(py, 2, 2, apply_y)

    for k in range(NSLOT):

        @pl.when(within(curve[k]))
        def _():
            block = send.at[pl.ds(k * SEND, SEND)]
            pltpu.make_async_copy(block, block, bulk_send.at[k]).wait()
            block = rest_send.at[pl.ds(2 * k, 2)]
            pltpu.make_async_copy(block, block, rest_sem_send.at[k]).wait()


def deliver(advanced, step, out, step_out, one, sem):
    copies = [
        pltpu.make_async_copy(
            advanced.at[c, pl.ds(8 * n, 8)], out.at[c, pl.ds(8 * n, 8)], sem.at[4 * c + n]
        )
        for c in range(NF) for n in range(4)
    ]
    for copy in copies:
        copy.start()
    one[...] = step[:, pl.ds(0, 1)]
    copies.append(pltpu.make_async_copy(one, step_out, sem.at[4 * NF]))
    copies[-1].start()
    for copy in copies:
        copy.wait()


def on_device(fields, patch_level, relation, face_half, neighbour, send_list):
    any_space = pl.BlockSpec(memory_space=pl.ANY)
    vmem = pl.BlockSpec(memory_space=pltpu.VMEM)
    cube = (NF, CELLS, CELLS, LANES)
    advanced, step = pl.pallas_call(
        body,
        out_shape=(pltpu.VMEM(cube, F32), pltpu.VMEM((1, LANES), F32)),
        in_specs=[any_space] * 6,
        out_specs=(vmem, vmem),
        scratch_shapes=[
            pltpu.VMEM((NF, PLANES, CELLS, LANES), F32),
            pltpu.VMEM((NF, PLANES, CELLS, LANES), F32),
            pltpu.VMEM(cube, F32),
            pltpu.VMEM(cube, F32),
            pltpu.VMEM((1, LANES), jnp.int32),
            pltpu.VMEM((4, LANES), jnp.int32),
            pltpu.VMEM((4, LANES), jnp.int32),
            pltpu.VMEM((4, 2, LANES), jnp.int32),
            pltpu.VMEM((SEND, NSLOT), jnp.int32),
            pltpu.VMEM((16 * ROWS, LANES), F32),
            pltpu.VMEM((256, LANES), F32),
            pltpu.VMEM((16 * ROWS, LANES), F32),
            pltpu.VMEM((256, LANES), F32),
            pltpu.VMEM((5 * LANES, LANES), F32),
            pltpu.VMEM((5 * LANES, LANES), F32),
            pltpu.VMEM((LANES, LANES), F32),
            pltpu.VMEM((LANES, TILES * LANES), F32),
            pltpu.VMEM((LANES, TILES * LANES), F32),
            pltpu.VMEM((REST, LANES), F32),
            pltpu.VMEM((REST, LANES), F32),
            pltpu.VMEM((48, LANES), F32),
            pltpu.VMEM((CELLS, LANES), F32),
            pltpu.VMEM((3, 1, LANES), F32),
            pltpu.VMEM((2 * NEAR_Z, 1, LANES), F32),
            pltpu.VMEM((2, 1, LANES), F32),
            pltpu.VMEM((2 * DIM_X * DIM_Y - 1, 1, LANES), F32),
            pltpu.SemaphoreType.DMA((2 * NF,)),
            pltpu.SemaphoreType.DMA((NF,)),
            pltpu.SemaphoreType.DMA((5,)),
            pltpu.SemaphoreType.DMA((NSLOT,)),
            pltpu.SemaphoreType.DMA((len(PARTS), NSLOT)),
            pltpu.SemaphoreType.DMA((NSLOT,)),
            pltpu.SemaphoreType.DMA((NSLOT,)),
            pltpu.SemaphoreType.DMA((3,)),
            pltpu.SemaphoreType.DMA((3,)),
        ],
        compiler_params=pltpu.CompilerParams(collective_id=0, has_side_effects=True),
    )(
        fields,
        patch_level.reshape(1, LANES),
        relation.T,
        face_half.T,
        jnp.transpose(neighbour, (1, 2, 0)),
        send_list[0].T,
    )
    advanced, step = pl.pallas_call(
        deliver,
        out_shape=(jax.ShapeDtypeStruct(cube, F32), jax.ShapeDtypeStruct((1, 1), F32)),
        in_specs=[vmem, vmem],
        out_specs=(any_space, any_space),
        scratch_shapes=[pltpu.VMEM((1, 1), F32), pltpu.SemaphoreType.DMA((4 * NF + 1,))],
    )(
        pltpu.with_memory_space_constraint(advanced, pltpu.VMEM),
        pltpu.with_memory_space_constraint(step, pltpu.VMEM),
    )
    return advanced, step.reshape(())


def solution(mesh):
    return jax.shard_map(
        on_device,
        mesh=mesh,
        in_specs=(
            P(None, None, None, "patch"),
            P("patch"),
            P("patch", None),
            P("patch", None),
            P("patch", None, None),
            P("patch", None, None),
        ),
        out_specs=(P(None, None, None, "patch"), P()),
        check_vma=False,
    )
```

```python
import jax
import jax.numpy as jnp
from jax import lax
from jax.experimental import pallas as pl
from jax.experimental.pallas import tpu as pltpu
from jax.sharding import PartitionSpec as P

MESH = pl.DeviceIdType.MESH
CELLS = 32
NF = 4
LANES = 128
HOPS = 8
SEND = 8
PLANES = CELLS + 4
ROWS = 80
NSLOT = 2 * HOPS
PARTS = ((0, 3), (3, 4), (7, 2))
TILES = 9
REST = 32
FAR_FIRST = [7, 15, 6, 14, 5, 13, 4, 12, 3, 11, 2, 10, 1, 9, 0, 8]
DIM_Y, DIM_X, DIM_Z = 4, 4, 16
NEAR_Z = 4
COURANT = 0.4
F32 = jnp.float32


def offsets():
    return [k + 1 for k in range(HOPS)] + [-(k + 1) for k in range(HOPS)]


def wave(depth):
    r = lax.rsqrt(depth)
    return r * r, depth * r


def physical(state, normal):
    inverse, root = wave(state[0])
    momentum = state[normal]
    velocity = momentum * inverse
    flux = [momentum, state[1] * velocity, state[2] * velocity, state[3] * velocity]
    flux[normal] = flux[normal] + 0.5 * (state[0] * state[0])
    return flux, jnp.abs(velocity) + root


def cell_sides(load, j):
    uppers, lowers = [], []
    for c in range(NF):
        here = load(c, j)
        delta = 0.25 * (load(c, j + 1) - load(c, j - 1))
        uppers.append(here + delta)
        lowers.append(here - delta)
    return uppers, lowers


def interface(left, left_flux, left_speed, right, right_flux, right_speed):
    widest = jnp.maximum(left_speed, right_speed)
    return [(left_flux[c] + right_flux[c]) - widest * (right[c] - left[c]) for c in range(NF)]


def body(fields, level, relation, half, near, sends, out, step_out,
         px, py, cx, cy, level_v, relation_v, half_v, near_v, sends_v,
         own, own0, far, far0, lean, far_lean, spare, send, recv, rest_send, rest_recv, edge, coarse, low, heard_z, heard_ends, heard_plane,
         edge_sem, load_sem, small_sem, bulk_send, bulk_recv, rest_sem_send, rest_sem_recv, low_send, low_recv, round_sem):
    me = lax.axis_index("patch")
    core = lax.rem(me, 2)
    z = lax.rem(me // 2, DIM_Z)
    x = lax.rem(me // (2 * DIM_Z), DIM_X)
    y = me // (2 * DIM_Z * DIM_X)
    total = DIM_Y * DIM_X * DIM_Z * 2

    def place(yy, xx, zz, cc):
        return ((yy * DIM_X + xx) * DIM_Z + zz) * 2 + cc

    def within(device):
        return jnp.logical_and(device >= 0, device < total)

    curve = [me + o for o in offsets()]
    sources = [me - o for o in offsets()]
    plane = [
        place(lax.rem(y + j, DIM_Y), lax.rem(x + k, DIM_X), z, cc)
        for j in range(DIM_Y) for k in range(DIM_X) for cc in (core, 1 - core)
    ][1:]
    beside = [
        place(y, lax.rem(x + 1, DIM_X), z, core),
        place(y, lax.rem(x + DIM_X - 1, DIM_X), z, core),
        place(lax.rem(y + 1, DIM_Y), x, z, core),
        place(lax.rem(y + DIM_Y - 1, DIM_Y), x, z, core),
        place(y, x, z, 1 - core),
    ]
    steps_z = [k for k in range(-NEAR_Z, NEAR_Z + 1) if k]
    along_z = [place(y, x, lax.rem(z + k + DIM_Z, DIM_Z), core) for k in steps_z]
    ends_z = [along_z[0], along_z[-1]]

    barrier = pltpu.get_barrier_semaphore()
    expected = len(beside) + len(along_z)
    for partner in curve:
        expected = expected + within(partner).astype(jnp.int32)

        @pl.when(within(partner))
        def _():
            pl.semaphore_signal(barrier, inc=1, device_id=(partner,), device_id_type=MESH)

    for partner in along_z + beside:
        pl.semaphore_signal(barrier, inc=1, device_id=(partner,), device_id_type=MESH)

    smalls = [
        pltpu.make_async_copy(source, target, small_sem.at[n])
        for n, (source, target) in enumerate(
            [(sends, sends_v), (level, level_v), (relation, relation_v), (half, half_v), (near, near_v)]
        )
    ]
    edges = [
        pltpu.make_async_copy(
            fields.at[c, pl.ds(first, 4)], px.at[c, pl.ds(first + 2, 4)], edge_sem.at[2 * c + first // 28]
        )
        for c in range(NF) for first in (0, CELLS - 4)
    ]
    middles = [
        pltpu.make_async_copy(
            fields.at[c, pl.ds(4, CELLS - 8)], px.at[c, pl.ds(6, CELLS - 8)], load_sem.at[c]
        )
        for c in range(NF)
    ]
    for copy in smalls + edges + middles:
        copy.start()

    px2 = px.reshape(NF * PLANES * CELLS, LANES)
    py2 = py.reshape(NF * PLANES * CELLS, LANES)
    out2 = out.reshape(NF * CELLS * CELLS, LANES)

    def restricted(ref, first, second):
        evens = ref[pl.ds(first, 16, stride=2), :] + ref[pl.ds(second, 16, stride=2), :]
        odds = ref[pl.ds(first + 1, 16, stride=2), :] + ref[pl.ds(second + 1, 16, stride=2), :]
        return 0.25 * (evens + odds)

    def pack(faces):
        for face in faces:
            planes = px2 if face < 2 else py2
            for c in range(NF):
                at = [(c * PLANES + (2 + k if face % 2 == 0 else 33 - k)) * CELLS for k in range(4)]
                row = (face * NF + c) * ROWS
                own[pl.ds(row, CELLS), :] = planes[pl.ds(at[0], CELLS), :]
                own[pl.ds(row + 32, CELLS), :] = planes[pl.ds(at[1], CELLS), :]
                own[pl.ds(row + 64, 16), :] = restricted(planes, at[2], at[3])
                own0[pl.ds((face * NF + c) * 16, 16), :] = restricted(planes, at[0], at[1])

    for copy in smalls + edges:
        copy.wait()
    pack((0, 1))

    lane = lax.broadcasted_iota(jnp.int32, (SEND, LANES), 1)
    slot = lax.broadcasted_iota(jnp.int32, (SEND, LANES), 0)
    listed = jnp.take_along_axis(jnp.concatenate([sends_v[...], jnp.zeros((SEND, LANES - NSLOT), jnp.int32)], axis=1), lane // SEND, axis=1)
    listed = jnp.sum(jnp.where(lax.rem(lane, SEND) == slot, listed, 0), axis=0, keepdims=True)
    listed = jnp.broadcast_to(listed, (LANES, LANES))
    def offer(tiles):
        for tile in tiles:
            columns = pl.ds(tile * LANES, LANES)
            rows = own[columns, :] if tile < 5 else lean[pl.ds((tile - 5) * LANES, LANES), :]
            send[:, columns] = jnp.take_along_axis(rows, listed, axis=1).T

    def thin():
        for face in (2, 3):
            for c in range(NF):
                row = (face * NF + c) * ROWS
                for g in range(2):
                    lean[pl.ds((face - 2) * 256 + (2 * c + g) * 28, 28), :] = own[pl.ds(row + 32 * g + 2, 28), :]
                lean[pl.ds((face - 2) * 256 + 224 + 8 * c, 8), :] = own[pl.ds(row + 66, 8), :]
                lean[pl.ds(512 + (face - 2) * 16 + 4 * c, 4), :] = own[pl.ds(row + 74, 4), :]

    group = lax.broadcasted_iota(jnp.int32, (REST, LANES), 1) // REST

    def offer_rest():
        spare[...] = jnp.take_along_axis(lean[pl.ds(4 * LANES, LANES), :], listed, axis=1).T
        merged = spare[pl.ds(0, REST, stride=4), :]
        for j in range(1, 4):
            merged = jnp.where(group == j, pltpu.roll(spare[pl.ds(j, REST, stride=4), :], j * REST, 1), merged)
        rest_send[...] = merged

    offer(range(5))
    for copy in middles:
        copy.wait()

    def scan_block(n, best):
        low_x, low_y = pl.multiple_of(n // 4 * 8, 8), pl.multiple_of(lax.rem(n, 4) * 8, 8)
        state = [px[c, pl.ds(low_x + 2, 8), pl.ds(low_y, 8), :] for c in range(NF)]
        for c in range(NF):
            py[c, pl.ds(low_y + 2, 8), pl.ds(low_x, 8), :] = jnp.swapaxes(state[c], 0, 1)
        inverse, root = wave(state[0])
        return jnp.maximum(best, jnp.maximum(jnp.abs(state[1]), jnp.abs(state[2])) * inverse + root)

    best = lax.fori_loop(0, 16, scan_block, jnp.zeros((8, 8, LANES), F32))
    top_speed = jnp.max(jnp.max(best, axis=0), axis=0, keepdims=True)
    spacing = lax.shift_left(jnp.ones((1, LANES), jnp.int32), 6 - level_v[...]).astype(F32)
    low[0] = spacing / top_speed

    def tell(value, targets, slots, stage):
        for n, target in enumerate(targets):
            pltpu.make_async_remote_copy(
                src_ref=value, dst_ref=slots.at[n], send_sem=low_send.at[stage], recv_sem=low_recv.at[stage],
                device_id=(target,), device_id_type=MESH,
            ).start()

    def hear(slots, stage):
        pltpu.make_async_copy(slots, slots, low_recv.at[stage]).wait()
        return jnp.min(slots[...], axis=0)

    def block_at(ref, part, k):
        return ref.at[pl.ds(k * SEND, SEND), pl.ds(PARTS[part][0] * LANES, PARTS[part][1] * LANES)]

    def exchange(part):
        for k in FAR_FIRST:

            @pl.when(within(curve[k]))
            def _():
                pltpu.make_async_remote_copy(
                    src_ref=block_at(send, part, k), dst_ref=block_at(recv, part, k), send_sem=bulk_send.at[k],
                    recv_sem=bulk_recv.at[part, k], device_id=(curve[k],), device_id_type=MESH,
                ).start()
                if part == 1:
                    rows = pl.ds(2 * k, 2)
                    pltpu.make_async_remote_copy(
                        src_ref=rest_send.at[rows], dst_ref=rest_recv.at[rows], send_sem=rest_sem_send.at[k],
                        recv_sem=rest_sem_recv.at[k], device_id=(curve[k],), device_id_type=MESH,
                    ).start()

    def arrived(part):
        for k in range(NSLOT):

            @pl.when(within(sources[k]))
            def _():
                block = block_at(recv, part, k)
                pltpu.make_async_copy(block, block, bulk_recv.at[part, k]).wait()
                if part == 1:
                    block = rest_recv.at[pl.ds(2 * k, 2)]
                    pltpu.make_async_copy(block, block, rest_sem_recv.at[k]).wait()

        first, count = PARTS[part]
        for tile in range(first, first + count):
            columns = pl.ds(tile * LANES, LANES)
            if tile < 5:
                far[columns, :] = recv[:, columns].T
            else:
                far_lean[pl.ds((tile - 5) * LANES, LANES), :] = recv[:, columns].T
        if part == 1:
            for j in range(4):
                spare[pl.ds(j, REST, stride=4), :] = pltpu.roll(rest_recv[...], (LANES - j * REST) % LANES, 1)
            far_lean[pl.ds(4 * LANES, LANES), :] = spare[...].T

    def relay(n):
        for partner in beside:
            pl.semaphore_signal(round_sem.at[n], inc=1, device_id=(partner,), device_id_type=MESH)

    def relayed(n):
        pl.semaphore_wait(round_sem.at[n], len(beside))

    pl.semaphore_wait(barrier, expected)
    tell(low.at[0], along_z, heard_z, 0)
    exchange(0)
    relay(0)

    pack((2, 3))
    thin()
    offer(range(5, TILES))
    offer_rest()
    relayed(0)
    relay(1)

    def interior(ref, normal, change):
        def row_tile(t, carry):
            rows = pl.ds(pl.multiple_of(t * 8, 8), 8)

            def load(c, j):
                return ref[c, j, rows, :]

            def advance(j, carried):
                left, left_flux, left_speed, before = carried
                upper, right = cell_sides(load, j + 1)
                right_flux, right_speed = physical(right, normal)
                flux = interface(left, left_flux, left_speed, right, right_flux, right_speed)
                for c in range(NF):
                    change[c, j - 2, rows, :] = flux[c] - before[c]
                upper_flux, upper_speed = physical(upper, normal)
                return upper, upper_flux, upper_speed, flux

            first, _ = cell_sides(load, 3)
            first_flux, first_speed = physical(first, normal)
            zero = jnp.zeros((8, LANES), F32)
            carried = advance(3, (first, first_flux, first_speed, [zero] * NF))
            last = lax.fori_loop(4, 32, advance, carried, unroll=4)
            for c in range(NF):
                change[c, 0, rows, :] = zero
                change[c, 30, rows, :] = -last[3][c]
                change[c, 31, rows, :] = zero
            return carry

        lax.fori_loop(0, 4, row_tile, 0)

    low[1] = jnp.minimum(low[0], hear(heard_z, 0))
    tell(low.at[1], ends_z, heard_ends, 1)
    for part in (1, 2):
        exchange(part)
    relayed(1)
    relay(2)

    interior(px, 1, cx)
    relayed(2)
    relay(3)
    interior(py, 2, cy)

    low[2] = jnp.minimum(low[1], hear(heard_ends, 1))
    relayed(3)
    tell(low.at[2], plane, heard_plane, 2)

    def corners():
        for face in (2, 3):
            for c in range(NF):
                row = (face * NF + c) * ROWS
                west, east = c * ROWS, (NF + c) * ROWS
                west0, east0 = c * 16, (NF + c) * 16
                for g in range(2):
                    side = g if face == 2 else 31 - g
                    for t, source in ((0, west), (1, west + 32), (30, east + 32), (31, east)):
                        far[pl.ds(row + 32 * g + t, 1), :] = far[pl.ds(source + side, 1), :]
                side = 1 if face == 2 else 14
                far[pl.ds(row + 64, 1), :] = far0[pl.ds(west0 + side, 1), :]
                far[pl.ds(row + 65, 1), :] = far[pl.ds(west + 64 + side, 1), :]
                far[pl.ds(row + 78, 1), :] = far[pl.ds(east + 64 + side, 1), :]
                far[pl.ds(row + 79, 1), :] = far0[pl.ds(east0 + side, 1), :]

    def fatten(face):
        for c in range(NF):
            row = (face * NF + c) * ROWS
            for g in range(2):
                far[pl.ds(row + 32 * g + 2, 28), :] = far_lean[pl.ds((face - 2) * 256 + (2 * c + g) * 28, 28), :]
            far[pl.ds(row + 66, 8), :] = far_lean[pl.ds((face - 2) * 256 + 224 + 8 * c, 8), :]
            far[pl.ds(row + 74, 4), :] = far_lean[pl.ds(512 + (face - 2) * 16 + 4 * c, 4), :]

    def shallow(face):
        for c in range(NF):
            row = (face * NF + c) * ROWS
            far0[pl.ds((face * NF + c) * 16, 16), :] = restricted(far, row, row + 32)

    def pick(mine, theirs, row, count, index):
        spot = jnp.broadcast_to(lax.rem(index, LANES), (count, LANES))
        remote = jnp.broadcast_to(index, (count, LANES)) >= LANES
        return jnp.where(
            remote,
            jnp.take_along_axis(theirs[pl.ds(row, count), :], spot, axis=1),
            jnp.take_along_axis(mine[pl.ds(row, count), :], spot, axis=1),
        )

    def ghosts(face):
        planes = px if face < 2 else py
        opposite = face ^ 1
        kind = jnp.broadcast_to(relation_v[pl.ds(face, 1), :], (CELLS, LANES))
        upper = jnp.broadcast_to(half_v[pl.ds(face, 1), :], (16, LANES)) == 1
        first = near_v[face, pl.ds(0, 1), :]
        second = near_v[face, pl.ds(1, 1), :]
        for c in range(NF):
            row = (opposite * NF + c) * ROWS
            row0 = (opposite * NF + c) * 16
            level_same = [pick(own, far, row + 32 * g, CELLS, first) for g in range(2)]
            finer = [
                jnp.concatenate([pick(own0, far0, row0, 16, first), pick(own0, far0, row0, 16, second)], axis=0),
                jnp.concatenate([pick(own, far, row + 64, 16, first), pick(own, far, row + 64, 16, second)], axis=0),
            ]
            value = level_same[0]
            edge[pl.ds(8, CELLS), :] = value
            edge[pl.ds(7, 1), :] = value[0:1]
            edge[pl.ds(40, 1), :] = value[31:32]
            slope = edge[pl.ds(9, CELLS), :] - edge[pl.ds(7, CELLS), :]
            base = jnp.where(upper, value[16:], value[:16])
            lean = 0.125 * jnp.where(upper, slope[16:], slope[:16])
            coarse[pl.ds(0, 16, stride=2), :] = base - lean
            coarse[pl.ds(1, 16, stride=2), :] = base + lean
            wide = coarse[...]
            sign = -1.0 if c == 1 + face // 2 else 1.0
            for g in range(2):
                mirror = sign * own[pl.ds((face * NF + c) * ROWS + 32 * g, CELLS), :]
                ghost = jnp.where(
                    kind == 0,
                    mirror,
                    jnp.where(kind == 1, level_same[g], jnp.where(kind == 2, wide, finer[g])),
                )
                planes[c, 1 - g if face % 2 == 0 else 34 + g] = ghost

    def rim(ref, normal, face, apply):
        start = 1 if face % 2 == 0 else 32

        def load(c, j):
            return ref[c, j]

        sides = [cell_sides(load, j) for j in (start, start + 1, start + 2)]
        flux = []
        for n in range(2):
            left, right = sides[n][0], sides[n + 1][1]
            left_flux, left_speed = physical(left, normal)
            right_flux, right_speed = physical(right, normal)
            flux.append(interface(left, left_flux, left_speed, right, right_flux, right_speed))
        for c in range(NF):
            if face % 2 == 0:
                apply(c, 0, flux[1][c] - flux[0][c])
                apply(c, 1, -flux[1][c])
            else:
                apply(c, 30, flux[0][c])
                apply(c, 31, flux[1][c] - flux[0][c])

    def apply_x(c, i, change):
        cx[c, i] = cx[c, i] + change

    def join(n, carry):
        low_x, low_y = pl.multiple_of(n // 4 * 8, 8), pl.multiple_of(lax.rem(n, 4) * 8, 8)
        for c in range(NF):
            turned = jnp.swapaxes(cy[c, pl.ds(low_y, 8), pl.ds(low_x, 8), :], 0, 1)
            at = (c, pl.ds(low_x, 8), pl.ds(low_y, 8))
            cx[at] = cx[at] + turned
        return carry

    lax.fori_loop(0, 16, join, 0)

    arrived(0)
    shallow(0)
    ghosts(1)
    rim(px, 1, 1, apply_x)
    lowest = jnp.minimum(low[2], hear(heard_plane, 2))
    time_step = COURANT * jnp.min(lowest, axis=1, keepdims=True)
    step_out[...] = jnp.broadcast_to(time_step, (1, LANES))
    ratio = jnp.broadcast_to(0.5 * (time_step / spacing), (CELLS, LANES))

    arrived(1)
    shallow(1)
    ghosts(0)
    rim(px, 1, 0, apply_x)
    corners()

    def settle(i, carry):
        for c in range(NF):
            out[c, i] = px[c, i + 2] - ratio * cx[c, i]
        return carry

    lax.fori_loop(0, CELLS, settle, 0, unroll=2)

    def apply_y(c, j, change):
        rows = pl.ds(c * CELLS * CELLS + j, CELLS, stride=CELLS)
        out2[rows, :] = out2[rows, :] - ratio * change

    for stage, slots in enumerate((heard_z, heard_ends, heard_plane)):
        pltpu.make_async_copy(slots, slots, low_send.at[stage]).wait()

    fatten(2)
    shallow(2)
    ghosts(3)
    rim(py, 2, 3, apply_y)
    arrived(2)
    fatten(3)
    shallow(3)
    ghosts(2)
    rim(py, 2, 2, apply_y)

    for k in range(NSLOT):

        @pl.when(within(curve[k]))
        def _():
            block = send.at[pl.ds(k * SEND, SEND)]
            pltpu.make_async_copy(block, block, bulk_send.at[k]).wait()
            block = rest_send.at[pl.ds(2 * k, 2)]
            pltpu.make_async_copy(block, block, rest_sem_send.at[k]).wait()


def deliver(advanced, step, out, step_out, one, sem):
    copies = [
        pltpu.make_async_copy(
            advanced.at[c, pl.ds(32 * n, 32)], out.at[c, pl.ds(32 * n, 32)], sem.at[1 * c + n]
        )
        for c in range(NF) for n in range(1)
    ]
    for copy in copies:
        copy.start()
    one[...] = step[:, pl.ds(0, 1)]
    copies.append(pltpu.make_async_copy(one, step_out, sem.at[1 * NF]))
    copies[-1].start()
    for copy in copies:
        copy.wait()


def on_device(fields, patch_level, relation, face_half, neighbour, send_list):
    any_space = pl.BlockSpec(memory_space=pl.ANY)
    vmem = pl.BlockSpec(memory_space=pltpu.VMEM)
    cube = (NF, CELLS, CELLS, LANES)
    advanced, step = pl.pallas_call(
        body,
        out_shape=(pltpu.VMEM(cube, F32), pltpu.VMEM((1, LANES), F32)),
        in_specs=[any_space] * 6,
        out_specs=(vmem, vmem),
        scratch_shapes=[
            pltpu.VMEM((NF, PLANES, CELLS, LANES), F32),
            pltpu.VMEM((NF, PLANES, CELLS, LANES), F32),
            pltpu.VMEM(cube, F32),
            pltpu.VMEM(cube, F32),
            pltpu.VMEM((1, LANES), jnp.int32),
            pltpu.VMEM((4, LANES), jnp.int32),
            pltpu.VMEM((4, LANES), jnp.int32),
            pltpu.VMEM((4, 2, LANES), jnp.int32),
            pltpu.VMEM((SEND, NSLOT), jnp.int32),
            pltpu.VMEM((16 * ROWS, LANES), F32),
            pltpu.VMEM((256, LANES), F32),
            pltpu.VMEM((16 * ROWS, LANES), F32),
            pltpu.VMEM((256, LANES), F32),
            pltpu.VMEM((5 * LANES, LANES), F32),
            pltpu.VMEM((5 * LANES, LANES), F32),
            pltpu.VMEM((LANES, LANES), F32),
            pltpu.VMEM((LANES, TILES * LANES), F32),
            pltpu.VMEM((LANES, TILES * LANES), F32),
            pltpu.VMEM((REST, LANES), F32),
            pltpu.VMEM((REST, LANES), F32),
            pltpu.VMEM((48, LANES), F32),
            pltpu.VMEM((CELLS, LANES), F32),
            pltpu.VMEM((3, 1, LANES), F32),
            pltpu.VMEM((2 * NEAR_Z, 1, LANES), F32),
            pltpu.VMEM((2, 1, LANES), F32),
            pltpu.VMEM((2 * DIM_X * DIM_Y - 1, 1, LANES), F32),
            pltpu.SemaphoreType.DMA((2 * NF,)),
            pltpu.SemaphoreType.DMA((NF,)),
            pltpu.SemaphoreType.DMA((5,)),
            pltpu.SemaphoreType.DMA((NSLOT,)),
            pltpu.SemaphoreType.DMA((len(PARTS), NSLOT)),
            pltpu.SemaphoreType.DMA((NSLOT,)),
            pltpu.SemaphoreType.DMA((NSLOT,)),
            pltpu.SemaphoreType.DMA((3,)),
            pltpu.SemaphoreType.DMA((3,)),
            pltpu.SemaphoreType.REGULAR((4,)),
        ],
        compiler_params=pltpu.CompilerParams(collective_id=0, has_side_effects=True),
    )(
        fields,
        patch_level.reshape(1, LANES),
        relation.T,
        face_half.T,
        jnp.transpose(neighbour, (1, 2, 0)),
        send_list[0].T,
    )
    advanced, step = pl.pallas_call(
        deliver,
        out_shape=(jax.ShapeDtypeStruct(cube, F32), jax.ShapeDtypeStruct((1, 1), F32)),
        in_specs=[vmem, vmem],
        out_specs=(any_space, any_space),
        scratch_shapes=[pltpu.VMEM((1, 1), F32), pltpu.SemaphoreType.DMA((1 * NF + 1,))],
    )(
        pltpu.with_memory_space_constraint(advanced, pltpu.VMEM),
        pltpu.with_memory_space_constraint(step, pltpu.VMEM),
    )
    return advanced, step.reshape(())


def solution(mesh):
    return jax.shard_map(
        on_device,
        mesh=mesh,
        in_specs=(
            P(None, None, None, "patch"),
            P("patch"),
            P("patch", None),
            P("patch", None),
            P("patch", None, None),
            P("patch", None, None),
        ),
        out_specs=(P(None, None, None, "patch"), P()),
        check_vma=False,
    )
```

```python
import jax
import jax.numpy as jnp
from jax import lax
from jax.experimental import pallas as pl
from jax.experimental.pallas import tpu as pltpu
from jax.sharding import PartitionSpec as P

MESH = pl.DeviceIdType.MESH
CELLS = 32
NF = 4
LANES = 128
HOPS = 8
SEND = 8
PLANES = CELLS + 4
ROWS = 80
NSLOT = 2 * HOPS
PARTS = ((0, 3), (3, 4), (7, 2))
TILES = 9
REST = 32
FAR_FIRST = [7, 15, 6, 14, 5, 13, 4, 12, 3, 11, 2, 10, 1, 9, 0, 8]
DIM_Y, DIM_X, DIM_Z = 4, 4, 16
NEAR_Z = 4
COURANT = 0.4
F32 = jnp.float32


def offsets():
    return [k + 1 for k in range(HOPS)] + [-(k + 1) for k in range(HOPS)]


def wave(depth):
    r = lax.rsqrt(depth)
    return r * r, depth * r


def physical(state, normal):
    inverse, root = wave(state[0])
    momentum = state[normal]
    velocity = momentum * inverse
    flux = [momentum, state[1] * velocity, state[2] * velocity, state[3] * velocity]
    flux[normal] = flux[normal] + 0.5 * (state[0] * state[0])
    return flux, jnp.abs(velocity) + root


def cell_sides(load, j):
    uppers, lowers = [], []
    for c in range(NF):
        here = load(c, j)
        delta = 0.25 * (load(c, j + 1) - load(c, j - 1))
        uppers.append(here + delta)
        lowers.append(here - delta)
    return uppers, lowers


def interface(left, left_flux, left_speed, right, right_flux, right_speed):
    widest = jnp.maximum(left_speed, right_speed)
    return [(left_flux[c] + right_flux[c]) - widest * (right[c] - left[c]) for c in range(NF)]


def body(fields, level, relation, half, near, sends, out, step_out,
         px, py, cx, cy, level_v, relation_v, half_v, near_v, sends_v,
         own, own0, far, far0, lean, far_lean, spare, send, recv, rest_send, rest_recv, edge, coarse, low, heard_z, heard_ends, heard_plane,
         edge_sem, load_sem, small_sem, bulk_send, bulk_recv, rest_sem_send, rest_sem_recv, low_send, low_recv, round_sem):
    me = lax.axis_index("patch")
    core = lax.rem(me, 2)
    z = lax.rem(me // 2, DIM_Z)
    x = lax.rem(me // (2 * DIM_Z), DIM_X)
    y = me // (2 * DIM_Z * DIM_X)
    total = DIM_Y * DIM_X * DIM_Z * 2

    def place(yy, xx, zz, cc):
        return ((yy * DIM_X + xx) * DIM_Z + zz) * 2 + cc

    def within(device):
        return jnp.logical_and(device >= 0, device < total)

    curve = [me + o for o in offsets()]
    sources = [me - o for o in offsets()]
    plane = [
        place(lax.rem(y + j, DIM_Y), lax.rem(x + k, DIM_X), z, cc)
        for j in range(DIM_Y) for k in range(DIM_X) for cc in (core, 1 - core)
    ][1:]
    beside = [
        place(y, lax.rem(x + 1, DIM_X), z, core),
        place(y, lax.rem(x + DIM_X - 1, DIM_X), z, core),
        place(lax.rem(y + 1, DIM_Y), x, z, core),
        place(lax.rem(y + DIM_Y - 1, DIM_Y), x, z, core),
        place(y, x, z, 1 - core),
    ]
    steps_z = [k for k in range(-NEAR_Z, NEAR_Z + 1) if k]
    along_z = [place(y, x, lax.rem(z + k + DIM_Z, DIM_Z), core) for k in steps_z]
    ends_z = [along_z[0], along_z[-1]]

    barrier = pltpu.get_barrier_semaphore()
    expected = len(beside) + len(along_z)
    for partner in curve:
        expected = expected + within(partner).astype(jnp.int32)

        @pl.when(within(partner))
        def _():
            pl.semaphore_signal(barrier, inc=1, device_id=(partner,), device_id_type=MESH)

    for partner in along_z + beside:
        pl.semaphore_signal(barrier, inc=1, device_id=(partner,), device_id_type=MESH)

    smalls = [
        pltpu.make_async_copy(source, target, small_sem.at[n])
        for n, (source, target) in enumerate(
            [(sends, sends_v), (level, level_v), (relation, relation_v), (half, half_v), (near, near_v)]
        )
    ]
    edges = [
        pltpu.make_async_copy(
            fields.at[c, pl.ds(first, 4)], px.at[c, pl.ds(first + 2, 4)], edge_sem.at[2 * c + first // 28]
        )
        for c in range(NF) for first in (0, CELLS - 4)
    ]
    middles = [
        pltpu.make_async_copy(
            fields.at[c, pl.ds(4, CELLS - 8)], px.at[c, pl.ds(6, CELLS - 8)], load_sem.at[c]
        )
        for c in range(NF)
    ]
    for copy in smalls + edges + middles:
        copy.start()

    px2 = px.reshape(NF * PLANES * CELLS, LANES)
    py2 = py.reshape(NF * PLANES * CELLS, LANES)
    out2 = out.reshape(NF * CELLS * CELLS, LANES)
    cx2 = cx.reshape(NF * CELLS * CELLS, LANES)

    def restricted(ref, first, second):
        evens = ref[pl.ds(first, 16, stride=2), :] + ref[pl.ds(second, 16, stride=2), :]
        odds = ref[pl.ds(first + 1, 16, stride=2), :] + ref[pl.ds(second + 1, 16, stride=2), :]
        return 0.25 * (evens + odds)

    def pack(faces):
        for face in faces:
            planes = px2 if face < 2 else py2
            for c in range(NF):
                at = [(c * PLANES + (2 + k if face % 2 == 0 else 33 - k)) * CELLS for k in range(4)]
                row = (face * NF + c) * ROWS
                own[pl.ds(row, CELLS), :] = planes[pl.ds(at[0], CELLS), :]
                own[pl.ds(row + 32, CELLS), :] = planes[pl.ds(at[1], CELLS), :]
                own[pl.ds(row + 64, 16), :] = restricted(planes, at[2], at[3])
                own0[pl.ds((face * NF + c) * 16, 16), :] = restricted(planes, at[0], at[1])

    for copy in smalls + edges:
        copy.wait()
    pack((0, 1))

    lane = lax.broadcasted_iota(jnp.int32, (SEND, LANES), 1)
    slot = lax.broadcasted_iota(jnp.int32, (SEND, LANES), 0)
    listed = jnp.take_along_axis(jnp.concatenate([sends_v[...], jnp.zeros((SEND, LANES - NSLOT), jnp.int32)], axis=1), lane // SEND, axis=1)
    listed = jnp.sum(jnp.where(lax.rem(lane, SEND) == slot, listed, 0), axis=0, keepdims=True)
    listed = jnp.broadcast_to(listed, (LANES, LANES))
    def offer(tiles):
        for tile in tiles:
            columns = pl.ds(tile * LANES, LANES)
            rows = own[columns, :] if tile < 5 else lean[pl.ds((tile - 5) * LANES, LANES), :]
            send[:, columns] = jnp.take_along_axis(rows, listed, axis=1).T

    def thin():
        for face in (2, 3):
            for c in range(NF):
                row = (face * NF + c) * ROWS
                for g in range(2):
                    lean[pl.ds((face - 2) * 256 + (2 * c + g) * 28, 28), :] = own[pl.ds(row + 32 * g + 2, 28), :]
                lean[pl.ds((face - 2) * 256 + 224 + 8 * c, 8), :] = own[pl.ds(row + 66, 8), :]
                lean[pl.ds(512 + (face - 2) * 16 + 4 * c, 4), :] = own[pl.ds(row + 74, 4), :]

    group = lax.broadcasted_iota(jnp.int32, (REST, LANES), 1) // REST

    def offer_rest():
        spare[...] = jnp.take_along_axis(lean[pl.ds(4 * LANES, LANES), :], listed, axis=1).T
        merged = spare[pl.ds(0, REST, stride=4), :]
        for j in range(1, 4):
            merged = jnp.where(group == j, pltpu.roll(spare[pl.ds(j, REST, stride=4), :], j * REST, 1), merged)
        rest_send[...] = merged

    offer(range(5))
    for copy in middles:
        copy.wait()

    def scan_block(n, best):
        low_x, low_y = pl.multiple_of(n // 4 * 8, 8), pl.multiple_of(lax.rem(n, 4) * 8, 8)
        state = [px[c, pl.ds(low_x + 2, 8), pl.ds(low_y, 8), :] for c in range(NF)]
        for c in range(NF):
            py[c, pl.ds(low_y + 2, 8), pl.ds(low_x, 8), :] = jnp.swapaxes(state[c], 0, 1)
        inverse, root = wave(state[0])
        return jnp.maximum(best, jnp.maximum(jnp.abs(state[1]), jnp.abs(state[2])) * inverse + root)

    best = lax.fori_loop(0, 16, scan_block, jnp.zeros((8, 8, LANES), F32))
    top_speed = jnp.max(jnp.max(best, axis=0), axis=0, keepdims=True)
    spacing = lax.shift_left(jnp.ones((1, LANES), jnp.int32), 6 - level_v[...]).astype(F32)
    low[0] = spacing / top_speed

    def tell(value, targets, slots, stage):
        for n, target in enumerate(targets):
            pltpu.make_async_remote_copy(
                src_ref=value, dst_ref=slots.at[n], send_sem=low_send.at[stage], recv_sem=low_recv.at[stage],
                device_id=(target,), device_id_type=MESH,
            ).start()

    def hear(slots, stage):
        pltpu.make_async_copy(slots, slots, low_recv.at[stage]).wait()
        return jnp.min(slots[...], axis=0)

    def block_at(ref, part, k):
        return ref.at[pl.ds(k * SEND, SEND), pl.ds(PARTS[part][0] * LANES, PARTS[part][1] * LANES)]

    def exchange(part):
        for k in FAR_FIRST:

            @pl.when(within(curve[k]))
            def _():
                pltpu.make_async_remote_copy(
                    src_ref=block_at(send, part, k), dst_ref=block_at(recv, part, k), send_sem=bulk_send.at[k],
                    recv_sem=bulk_recv.at[part, k], device_id=(curve[k],), device_id_type=MESH,
                ).start()
                if part == 1:
                    rows = pl.ds(2 * k, 2)
                    pltpu.make_async_remote_copy(
                        src_ref=rest_send.at[rows], dst_ref=rest_recv.at[rows], send_sem=rest_sem_send.at[k],
                        recv_sem=rest_sem_recv.at[k], device_id=(curve[k],), device_id_type=MESH,
                    ).start()

    def arrived(part):
        for k in range(NSLOT):

            @pl.when(within(sources[k]))
            def _():
                block = block_at(recv, part, k)
                pltpu.make_async_copy(block, block, bulk_recv.at[part, k]).wait()
                if part == 1:
                    block = rest_recv.at[pl.ds(2 * k, 2)]
                    pltpu.make_async_copy(block, block, rest_sem_recv.at[k]).wait()

        first, count = PARTS[part]
        for tile in range(first, first + count):
            columns = pl.ds(tile * LANES, LANES)
            if tile < 5:
                far[columns, :] = recv[:, columns].T
            else:
                far_lean[pl.ds((tile - 5) * LANES, LANES), :] = recv[:, columns].T
        if part == 1:
            for j in range(4):
                spare[pl.ds(j, REST, stride=4), :] = pltpu.roll(rest_recv[...], (LANES - j * REST) % LANES, 1)
            far_lean[pl.ds(4 * LANES, LANES), :] = spare[...].T

    def relay(n):
        for partner in beside:
            pl.semaphore_signal(round_sem.at[n], inc=1, device_id=(partner,), device_id_type=MESH)

    def relayed(n):
        pl.semaphore_wait(round_sem.at[n], len(beside))

    pl.semaphore_wait(barrier, expected)
    tell(low.at[0], along_z, heard_z, 0)
    exchange(0)
    relay(0)

    pack((2, 3))
    thin()
    offer(range(5, TILES))
    offer_rest()
    relayed(0)
    relay(1)

    def interior(ref, normal, change):
        def row_tile(t, carry):
            rows = pl.ds(pl.multiple_of(t * 8, 8), 8)

            def load(c, j):
                return ref[c, j, rows, :]

            def advance(j, carried):
                left, left_flux, left_speed, before = carried
                upper, right = cell_sides(load, j + 1)
                right_flux, right_speed = physical(right, normal)
                flux = interface(left, left_flux, left_speed, right, right_flux, right_speed)
                for c in range(NF):
                    change[c, j - 2, rows, :] = flux[c] - before[c]
                upper_flux, upper_speed = physical(upper, normal)
                return upper, upper_flux, upper_speed, flux

            first, _ = cell_sides(load, 3)
            first_flux, first_speed = physical(first, normal)
            zero = jnp.zeros((8, LANES), F32)
            carried = advance(3, (first, first_flux, first_speed, [zero] * NF))
            last = lax.fori_loop(4, 32, advance, carried, unroll=4)
            for c in range(NF):
                change[c, 0, rows, :] = zero
                change[c, 30, rows, :] = -last[3][c]
                change[c, 31, rows, :] = zero
            return carry

        lax.fori_loop(0, 4, row_tile, 0)

    low[1] = jnp.minimum(low[0], hear(heard_z, 0))
    tell(low.at[1], ends_z, heard_ends, 1)
    for part in (1, 2):
        exchange(part)
    relayed(1)
    relay(2)

    interior(px, 1, cx)
    relayed(2)
    relay(3)
    interior(py, 2, cy)

    low[2] = jnp.minimum(low[1], hear(heard_ends, 1))
    relayed(3)
    tell(low.at[2], plane, heard_plane, 2)

    def corners():
        for face in (2, 3):
            for c in range(NF):
                row = (face * NF + c) * ROWS
                west, east = c * ROWS, (NF + c) * ROWS
                west0, east0 = c * 16, (NF + c) * 16
                for g in range(2):
                    side = g if face == 2 else 31 - g
                    for t, source in ((0, west), (1, west + 32), (30, east + 32), (31, east)):
                        far[pl.ds(row + 32 * g + t, 1), :] = far[pl.ds(source + side, 1), :]
                side = 1 if face == 2 else 14
                far[pl.ds(row + 64, 1), :] = far0[pl.ds(west0 + side, 1), :]
                far[pl.ds(row + 65, 1), :] = far[pl.ds(west + 64 + side, 1), :]
                far[pl.ds(row + 78, 1), :] = far[pl.ds(east + 64 + side, 1), :]
                far[pl.ds(row + 79, 1), :] = far0[pl.ds(east0 + side, 1), :]

    def fatten(face):
        for c in range(NF):
            row = (face * NF + c) * ROWS
            for g in range(2):
                far[pl.ds(row + 32 * g + 2, 28), :] = far_lean[pl.ds((face - 2) * 256 + (2 * c + g) * 28, 28), :]
            far[pl.ds(row + 66, 8), :] = far_lean[pl.ds((face - 2) * 256 + 224 + 8 * c, 8), :]
            far[pl.ds(row + 74, 4), :] = far_lean[pl.ds(512 + (face - 2) * 16 + 4 * c, 4), :]

    def shallow(face):
        for c in range(NF):
            row = (face * NF + c) * ROWS
            far0[pl.ds((face * NF + c) * 16, 16), :] = restricted(far, row, row + 32)

    def pick(mine, theirs, row, count, index):
        spot = jnp.broadcast_to(lax.rem(index, LANES), (count, LANES))
        remote = jnp.broadcast_to(index, (count, LANES)) >= LANES
        return jnp.where(
            remote,
            jnp.take_along_axis(theirs[pl.ds(row, count), :], spot, axis=1),
            jnp.take_along_axis(mine[pl.ds(row, count), :], spot, axis=1),
        )

    def ghosts(face):
        planes = px if face < 2 else py
        opposite = face ^ 1
        kind = jnp.broadcast_to(relation_v[pl.ds(face, 1), :], (CELLS, LANES))
        upper = jnp.broadcast_to(half_v[pl.ds(face, 1), :], (16, LANES)) == 1
        first = near_v[face, pl.ds(0, 1), :]
        second = near_v[face, pl.ds(1, 1), :]
        for c in range(NF):
            row = (opposite * NF + c) * ROWS
            row0 = (opposite * NF + c) * 16
            level_same = [pick(own, far, row + 32 * g, CELLS, first) for g in range(2)]
            finer = [
                jnp.concatenate([pick(own0, far0, row0, 16, first), pick(own0, far0, row0, 16, second)], axis=0),
                jnp.concatenate([pick(own, far, row + 64, 16, first), pick(own, far, row + 64, 16, second)], axis=0),
            ]
            value = level_same[0]
            edge[pl.ds(8, CELLS), :] = value
            edge[pl.ds(7, 1), :] = value[0:1]
            edge[pl.ds(40, 1), :] = value[31:32]
            slope = edge[pl.ds(9, CELLS), :] - edge[pl.ds(7, CELLS), :]
            base = jnp.where(upper, value[16:], value[:16])
            lean = 0.125 * jnp.where(upper, slope[16:], slope[:16])
            coarse[pl.ds(0, 16, stride=2), :] = base - lean
            coarse[pl.ds(1, 16, stride=2), :] = base + lean
            wide = coarse[...]
            sign = -1.0 if c == 1 + face // 2 else 1.0
            for g in range(2):
                mirror = sign * own[pl.ds((face * NF + c) * ROWS + 32 * g, CELLS), :]
                ghost = jnp.where(
                    kind == 0,
                    mirror,
                    jnp.where(kind == 1, level_same[g], jnp.where(kind == 2, wide, finer[g])),
                )
                planes[c, 1 - g if face % 2 == 0 else 34 + g] = ghost

    def rim(ref, normal, face, apply):
        start = 1 if face % 2 == 0 else 32

        def load(c, j):
            return ref[c, j]

        sides = [cell_sides(load, j) for j in (start, start + 1, start + 2)]
        flux = []
        for n in range(2):
            left, right = sides[n][0], sides[n + 1][1]
            left_flux, left_speed = physical(left, normal)
            right_flux, right_speed = physical(right, normal)
            flux.append(interface(left, left_flux, left_speed, right, right_flux, right_speed))
        for c in range(NF):
            if face % 2 == 0:
                apply(c, 0, flux[1][c] - flux[0][c])
                apply(c, 1, -flux[1][c])
            else:
                apply(c, 30, flux[0][c])
                apply(c, 31, flux[1][c] - flux[0][c])

    def apply_x(c, i, change):
        cx[c, i] = cx[c, i] + change

    def join(n, carry):
        low_x, low_y = pl.multiple_of(n // 4 * 8, 8), pl.multiple_of(lax.rem(n, 4) * 8, 8)
        for c in range(NF):
            turned = jnp.swapaxes(cy[c, pl.ds(low_y, 8), pl.ds(low_x, 8), :], 0, 1)
            at = (c, pl.ds(low_x, 8), pl.ds(low_y, 8))
            cx[at] = cx[at] + turned
        return carry

    lax.fori_loop(0, 16, join, 0)

    arrived(0)
    shallow(0)
    ghosts(1)
    rim(px, 1, 1, apply_x)
    def apply_y(c, j, change):
        rows = pl.ds(c * CELLS * CELLS + j, CELLS, stride=CELLS)
        cx2[rows, :] = cx2[rows, :] + change

    arrived(1)
    shallow(1)
    ghosts(0)
    rim(px, 1, 0, apply_x)
    corners()
    fatten(2)
    shallow(2)
    ghosts(3)
    rim(py, 2, 3, apply_y)

    lowest = jnp.minimum(low[2], hear(heard_plane, 2))
    time_step = COURANT * jnp.min(lowest, axis=1, keepdims=True)
    step_out[...] = jnp.broadcast_to(time_step, (1, LANES))
    ratio = jnp.broadcast_to(0.5 * (time_step / spacing), (CELLS, LANES))

    def settle(i, carry):
        for c in range(NF):
            out[c, i] = px[c, i + 2] - ratio * cx[c, i]
        return carry

    lax.fori_loop(0, CELLS, settle, 0, unroll=2)

    for stage, slots in enumerate((heard_z, heard_ends, heard_plane)):
        pltpu.make_async_copy(slots, slots, low_send.at[stage]).wait()

    def settled_y(c, j, change):
        rows = pl.ds(c * CELLS * CELLS + j, CELLS, stride=CELLS)
        out2[rows, :] = out2[rows, :] - ratio * change

    arrived(2)
    fatten(3)
    shallow(3)
    ghosts(2)
    rim(py, 2, 2, settled_y)

    for k in range(NSLOT):

        @pl.when(within(curve[k]))
        def _():
            block = send.at[pl.ds(k * SEND, SEND)]
            pltpu.make_async_copy(block, block, bulk_send.at[k]).wait()
            block = rest_send.at[pl.ds(2 * k, 2)]
            pltpu.make_async_copy(block, block, rest_sem_send.at[k]).wait()


def deliver(advanced, step, out, step_out, one, sem):
    copies = [
        pltpu.make_async_copy(
            advanced.at[c, pl.ds(32 * n, 32)], out.at[c, pl.ds(32 * n, 32)], sem.at[1 * c + n]
        )
        for c in range(NF) for n in range(1)
    ]
    for copy in copies:
        copy.start()
    one[...] = step[:, pl.ds(0, 1)]
    copies.append(pltpu.make_async_copy(one, step_out, sem.at[1 * NF]))
    copies[-1].start()
    for copy in copies:
        copy.wait()


def on_device(fields, patch_level, relation, face_half, neighbour, send_list):
    any_space = pl.BlockSpec(memory_space=pl.ANY)
    vmem = pl.BlockSpec(memory_space=pltpu.VMEM)
    cube = (NF, CELLS, CELLS, LANES)
    advanced, step = pl.pallas_call(
        body,
        out_shape=(pltpu.VMEM(cube, F32), pltpu.VMEM((1, LANES), F32)),
        in_specs=[any_space] * 6,
        out_specs=(vmem, vmem),
        scratch_shapes=[
            pltpu.VMEM((NF, PLANES, CELLS, LANES), F32),
            pltpu.VMEM((NF, PLANES, CELLS, LANES), F32),
            pltpu.VMEM(cube, F32),
            pltpu.VMEM(cube, F32),
            pltpu.VMEM((1, LANES), jnp.int32),
            pltpu.VMEM((4, LANES), jnp.int32),
            pltpu.VMEM((4, LANES), jnp.int32),
            pltpu.VMEM((4, 2, LANES), jnp.int32),
            pltpu.VMEM((SEND, NSLOT), jnp.int32),
            pltpu.VMEM((16 * ROWS, LANES), F32),
            pltpu.VMEM((256, LANES), F32),
            pltpu.VMEM((16 * ROWS, LANES), F32),
            pltpu.VMEM((256, LANES), F32),
            pltpu.VMEM((5 * LANES, LANES), F32),
            pltpu.VMEM((5 * LANES, LANES), F32),
            pltpu.VMEM((LANES, LANES), F32),
            pltpu.VMEM((LANES, TILES * LANES), F32),
            pltpu.VMEM((LANES, TILES * LANES), F32),
            pltpu.VMEM((REST, LANES), F32),
            pltpu.VMEM((REST, LANES), F32),
            pltpu.VMEM((48, LANES), F32),
            pltpu.VMEM((CELLS, LANES), F32),
            pltpu.VMEM((3, 1, LANES), F32),
            pltpu.VMEM((2 * NEAR_Z, 1, LANES), F32),
            pltpu.VMEM((2, 1, LANES), F32),
            pltpu.VMEM((2 * DIM_X * DIM_Y - 1, 1, LANES), F32),
            pltpu.SemaphoreType.DMA((2 * NF,)),
            pltpu.SemaphoreType.DMA((NF,)),
            pltpu.SemaphoreType.DMA((5,)),
            pltpu.SemaphoreType.DMA((NSLOT,)),
            pltpu.SemaphoreType.DMA((len(PARTS), NSLOT)),
            pltpu.SemaphoreType.DMA((NSLOT,)),
            pltpu.SemaphoreType.DMA((NSLOT,)),
            pltpu.SemaphoreType.DMA((3,)),
            pltpu.SemaphoreType.DMA((3,)),
            pltpu.SemaphoreType.REGULAR((4,)),
        ],
        compiler_params=pltpu.CompilerParams(collective_id=0, has_side_effects=True),
    )(
        fields,
        patch_level.reshape(1, LANES),
        relation.T,
        face_half.T,
        jnp.transpose(neighbour, (1, 2, 0)),
        send_list[0].T,
    )
    advanced, step = pl.pallas_call(
        deliver,
        out_shape=(jax.ShapeDtypeStruct(cube, F32), jax.ShapeDtypeStruct((1, 1), F32)),
        in_specs=[vmem, vmem],
        out_specs=(any_space, any_space),
        scratch_shapes=[pltpu.VMEM((1, 1), F32), pltpu.SemaphoreType.DMA((1 * NF + 1,))],
    )(
        pltpu.with_memory_space_constraint(advanced, pltpu.VMEM),
        pltpu.with_memory_space_constraint(step, pltpu.VMEM),
    )
    return advanced, step.reshape(())


def solution(mesh):
    return jax.shard_map(
        on_device,
        mesh=mesh,
        in_specs=(
            P(None, None, None, "patch"),
            P("patch"),
            P("patch", None),
            P("patch", None),
            P("patch", None, None),
            P("patch", None, None),
        ),
        out_specs=(P(None, None, None, "patch"), P()),
        check_vma=False,
    )
```

```python
import jax
import jax.numpy as jnp
from jax import lax
from jax.experimental import pallas as pl
from jax.experimental.pallas import tpu as pltpu
from jax.sharding import PartitionSpec as P

MESH = pl.DeviceIdType.MESH
CELLS = 32
NF = 4
LANES = 128
HOPS = 8
SEND = 8
PLANES = CELLS + 4
ROWS = 80
NSLOT = 2 * HOPS
PARTS = ((0, 3), (3, 4), (7, 2))
TILES = 9
REST = 32
FAR_FIRST = [7, 15, 6, 14, 5, 13, 4, 12, 3, 11, 2, 10, 1, 9, 0, 8]
DIM_Y, DIM_X, DIM_Z = 4, 4, 16
NEAR_Z = 4
COURANT = 0.4
F32 = jnp.float32


def offsets():
    return [k + 1 for k in range(HOPS)] + [-(k + 1) for k in range(HOPS)]


def wave(depth):
    r = lax.rsqrt(depth)
    return r * r, depth * r


def physical(state, normal):
    inverse, root = wave(state[0])
    momentum = state[normal]
    velocity = momentum * inverse
    flux = [momentum, state[1] * velocity, state[2] * velocity, state[3] * velocity]
    flux[normal] = flux[normal] + 0.5 * (state[0] * state[0])
    return flux, jnp.abs(velocity) + root


def cell_sides(load, j):
    uppers, lowers = [], []
    for c in range(NF):
        here = load(c, j)
        delta = 0.25 * (load(c, j + 1) - load(c, j - 1))
        uppers.append(here + delta)
        lowers.append(here - delta)
    return uppers, lowers


def interface(left, left_flux, left_speed, right, right_flux, right_speed):
    widest = jnp.maximum(left_speed, right_speed)
    return [(left_flux[c] + right_flux[c]) - widest * (right[c] - left[c]) for c in range(NF)]


def ghost_maker(own, own0, far, far0, relation_v, half_v, near_v, edge, coarse):
    def pick(mine, theirs, row, count, index):
        spot = jnp.broadcast_to(lax.rem(index, LANES), (count, LANES))
        remote = jnp.broadcast_to(index, (count, LANES)) >= LANES
        return jnp.where(
            remote,
            jnp.take_along_axis(theirs[pl.ds(row, count), :], spot, axis=1),
            jnp.take_along_axis(mine[pl.ds(row, count), :], spot, axis=1),
        )

    def ghosts(face, store):
        opposite = face ^ 1
        kind = jnp.broadcast_to(relation_v[pl.ds(face, 1), :], (CELLS, LANES))
        upper = jnp.broadcast_to(half_v[pl.ds(face, 1), :], (16, LANES)) == 1
        first = near_v[face, pl.ds(0, 1), :]
        second = near_v[face, pl.ds(1, 1), :]
        for c in range(NF):
            row = (opposite * NF + c) * ROWS
            row0 = (opposite * NF + c) * 16
            level_same = [pick(own, far, row + 32 * g, CELLS, first) for g in range(2)]
            finer = [
                jnp.concatenate([pick(own0, far0, row0, 16, first), pick(own0, far0, row0, 16, second)], axis=0),
                jnp.concatenate([pick(own, far, row + 64, 16, first), pick(own, far, row + 64, 16, second)], axis=0),
            ]
            value = level_same[0]
            edge[pl.ds(8, CELLS), :] = value
            edge[pl.ds(7, 1), :] = value[0:1]
            edge[pl.ds(40, 1), :] = value[31:32]
            slope = edge[pl.ds(9, CELLS), :] - edge[pl.ds(7, CELLS), :]
            base = jnp.where(upper, value[16:], value[:16])
            lean = 0.125 * jnp.where(upper, slope[16:], slope[:16])
            coarse[pl.ds(0, 16, stride=2), :] = base - lean
            coarse[pl.ds(1, 16, stride=2), :] = base + lean
            wide = coarse[...]
            sign = -1.0 if c == 1 + face // 2 else 1.0
            for g in range(2):
                mirror = sign * own[pl.ds((face * NF + c) * ROWS + 32 * g, CELLS), :]
                ghost = jnp.where(
                    kind == 0,
                    mirror,
                    jnp.where(kind == 1, level_same[g], jnp.where(kind == 2, wide, finer[g])),
                )
                store(c, 1 - g if face % 2 == 0 else 34 + g, ghost)

    return ghosts


def rim(load, normal, face, apply):
    start = 1 if face % 2 == 0 else 32

    sides = [cell_sides(load, j) for j in (start, start + 1, start + 2)]
    flux = []
    for n in range(2):
        left, right = sides[n][0], sides[n + 1][1]
        left_flux, left_speed = physical(left, normal)
        right_flux, right_speed = physical(right, normal)
        flux.append(interface(left, left_flux, left_speed, right, right_flux, right_speed))
    for c in range(NF):
        if face % 2 == 0:
            apply(c, 0, flux[1][c] - flux[0][c])
            apply(c, 1, -flux[1][c])
        else:
            apply(c, 30, flux[0][c])
            apply(c, 31, flux[1][c] - flux[0][c])


def body(fields, level, relation, half, near, sends,
         out, step_out, ratio_out, py, own, own0, far, far0, relation_v, half_v, near_v,
         px, cx, cy, level_v, sends_v, lean, far_lean, spare, send, recv, rest_send, rest_recv, edge, coarse, low, heard_z, heard_ends, heard_plane,
         edge_sem, load_sem, small_sem, bulk_send, bulk_recv, rest_sem_send, rest_sem_recv, low_send, low_recv, round_sem):
    me = lax.axis_index("patch")
    core = lax.rem(me, 2)
    z = lax.rem(me // 2, DIM_Z)
    x = lax.rem(me // (2 * DIM_Z), DIM_X)
    y = me // (2 * DIM_Z * DIM_X)
    total = DIM_Y * DIM_X * DIM_Z * 2

    def place(yy, xx, zz, cc):
        return ((yy * DIM_X + xx) * DIM_Z + zz) * 2 + cc

    def within(device):
        return jnp.logical_and(device >= 0, device < total)

    curve = [me + o for o in offsets()]
    sources = [me - o for o in offsets()]
    plane = [
        place(lax.rem(y + j, DIM_Y), lax.rem(x + k, DIM_X), z, cc)
        for j in range(DIM_Y) for k in range(DIM_X) for cc in (core, 1 - core)
    ][1:]
    beside = [
        place(y, lax.rem(x + 1, DIM_X), z, core),
        place(y, lax.rem(x + DIM_X - 1, DIM_X), z, core),
        place(lax.rem(y + 1, DIM_Y), x, z, core),
        place(lax.rem(y + DIM_Y - 1, DIM_Y), x, z, core),
        place(y, x, z, 1 - core),
    ]
    steps_z = [k for k in range(-NEAR_Z, NEAR_Z + 1) if k]
    along_z = [place(y, x, lax.rem(z + k + DIM_Z, DIM_Z), core) for k in steps_z]
    ends_z = [along_z[0], along_z[-1]]

    barrier = pltpu.get_barrier_semaphore()
    expected = len(beside) + len(along_z)
    for partner in curve:
        expected = expected + within(partner).astype(jnp.int32)

        @pl.when(within(partner))
        def _():
            pl.semaphore_signal(barrier, inc=1, device_id=(partner,), device_id_type=MESH)

    for partner in along_z + beside:
        pl.semaphore_signal(barrier, inc=1, device_id=(partner,), device_id_type=MESH)

    smalls = [
        pltpu.make_async_copy(source, target, small_sem.at[n])
        for n, (source, target) in enumerate(
            [(sends, sends_v), (level, level_v), (relation, relation_v), (half, half_v), (near, near_v)]
        )
    ]
    edges = [
        pltpu.make_async_copy(
            fields.at[c, pl.ds(first, 4)], px.at[c, pl.ds(first + 2, 4)], edge_sem.at[2 * c + first // 28]
        )
        for c in range(NF) for first in (0, CELLS - 4)
    ]
    middles = [
        pltpu.make_async_copy(
            fields.at[c, pl.ds(4, CELLS - 8)], px.at[c, pl.ds(6, CELLS - 8)], load_sem.at[c]
        )
        for c in range(NF)
    ]
    for copy in smalls + edges + middles:
        copy.start()

    px2 = px.reshape(NF * PLANES * CELLS, LANES)
    py2 = py.reshape(NF * PLANES * CELLS, LANES)
    cx2 = cx.reshape(NF * CELLS * CELLS, LANES)

    def restricted(ref, first, second):
        evens = ref[pl.ds(first, 16, stride=2), :] + ref[pl.ds(second, 16, stride=2), :]
        odds = ref[pl.ds(first + 1, 16, stride=2), :] + ref[pl.ds(second + 1, 16, stride=2), :]
        return 0.25 * (evens + odds)

    def pack(faces):
        for face in faces:
            planes = px2 if face < 2 else py2
            for c in range(NF):
                at = [(c * PLANES + (2 + k if face % 2 == 0 else 33 - k)) * CELLS for k in range(4)]
                row = (face * NF + c) * ROWS
                own[pl.ds(row, CELLS), :] = planes[pl.ds(at[0], CELLS), :]
                own[pl.ds(row + 32, CELLS), :] = planes[pl.ds(at[1], CELLS), :]
                own[pl.ds(row + 64, 16), :] = restricted(planes, at[2], at[3])
                own0[pl.ds((face * NF + c) * 16, 16), :] = restricted(planes, at[0], at[1])

    for copy in smalls + edges:
        copy.wait()
    pack((0, 1))

    lane = lax.broadcasted_iota(jnp.int32, (SEND, LANES), 1)
    slot = lax.broadcasted_iota(jnp.int32, (SEND, LANES), 0)
    listed = jnp.take_along_axis(jnp.concatenate([sends_v[...], jnp.zeros((SEND, LANES - NSLOT), jnp.int32)], axis=1), lane // SEND, axis=1)
    listed = jnp.sum(jnp.where(lax.rem(lane, SEND) == slot, listed, 0), axis=0, keepdims=True)
    listed = jnp.broadcast_to(listed, (LANES, LANES))
    def offer(tiles):
        for tile in tiles:
            columns = pl.ds(tile * LANES, LANES)
            rows = own[columns, :] if tile < 5 else lean[pl.ds((tile - 5) * LANES, LANES), :]
            send[:, columns] = jnp.take_along_axis(rows, listed, axis=1).T

    def thin():
        for face in (2, 3):
            for c in range(NF):
                row = (face * NF + c) * ROWS
                for g in range(2):
                    lean[pl.ds((face - 2) * 256 + (2 * c + g) * 28, 28), :] = own[pl.ds(row + 32 * g + 2, 28), :]
                lean[pl.ds((face - 2) * 256 + 224 + 8 * c, 8), :] = own[pl.ds(row + 66, 8), :]
                lean[pl.ds(512 + (face - 2) * 16 + 4 * c, 4), :] = own[pl.ds(row + 74, 4), :]

    group = lax.broadcasted_iota(jnp.int32, (REST, LANES), 1) // REST

    def offer_rest():
        spare[...] = jnp.take_along_axis(lean[pl.ds(4 * LANES, LANES), :], listed, axis=1).T
        merged = spare[pl.ds(0, REST, stride=4), :]
        for j in range(1, 4):
            merged = jnp.where(group == j, pltpu.roll(spare[pl.ds(j, REST, stride=4), :], j * REST, 1), merged)
        rest_send[...] = merged

    offer(range(5))
    for copy in middles:
        copy.wait()

    def scan_block(n, best):
        low_x, low_y = pl.multiple_of(n // 4 * 8, 8), pl.multiple_of(lax.rem(n, 4) * 8, 8)
        state = [px[c, pl.ds(low_x + 2, 8), pl.ds(low_y, 8), :] for c in range(NF)]
        for c in range(NF):
            py[c, pl.ds(low_y + 2, 8), pl.ds(low_x, 8), :] = jnp.swapaxes(state[c], 0, 1)
        inverse, root = wave(state[0])
        return jnp.maximum(best, jnp.maximum(jnp.abs(state[1]), jnp.abs(state[2])) * inverse + root)

    best = lax.fori_loop(0, 16, scan_block, jnp.zeros((8, 8, LANES), F32))
    top_speed = jnp.max(jnp.max(best, axis=0), axis=0, keepdims=True)
    spacing = lax.shift_left(jnp.ones((1, LANES), jnp.int32), 6 - level_v[...]).astype(F32)
    low[0] = spacing / top_speed

    def tell(value, targets, slots, stage):
        for n, target in enumerate(targets):
            pltpu.make_async_remote_copy(
                src_ref=value, dst_ref=slots.at[n], send_sem=low_send.at[stage], recv_sem=low_recv.at[stage],
                device_id=(target,), device_id_type=MESH,
            ).start()

    def hear(slots, stage):
        pltpu.make_async_copy(slots, slots, low_recv.at[stage]).wait()
        return jnp.min(slots[...], axis=0)

    def block_at(ref, part, k):
        return ref.at[pl.ds(k * SEND, SEND), pl.ds(PARTS[part][0] * LANES, PARTS[part][1] * LANES)]

    def exchange(part):
        for k in FAR_FIRST:

            @pl.when(within(curve[k]))
            def _():
                pltpu.make_async_remote_copy(
                    src_ref=block_at(send, part, k), dst_ref=block_at(recv, part, k), send_sem=bulk_send.at[k],
                    recv_sem=bulk_recv.at[part, k], device_id=(curve[k],), device_id_type=MESH,
                ).start()
                if part == 1:
                    rows = pl.ds(2 * k, 2)
                    pltpu.make_async_remote_copy(
                        src_ref=rest_send.at[rows], dst_ref=rest_recv.at[rows], send_sem=rest_sem_send.at[k],
                        recv_sem=rest_sem_recv.at[k], device_id=(curve[k],), device_id_type=MESH,
                    ).start()

    def arrived(part):
        for k in range(NSLOT):

            @pl.when(within(sources[k]))
            def _():
                block = block_at(recv, part, k)
                pltpu.make_async_copy(block, block, bulk_recv.at[part, k]).wait()
                if part == 1:
                    block = rest_recv.at[pl.ds(2 * k, 2)]
                    pltpu.make_async_copy(block, block, rest_sem_recv.at[k]).wait()

        first, count = PARTS[part]
        for tile in range(first, first + count):
            columns = pl.ds(tile * LANES, LANES)
            if tile < 5:
                far[columns, :] = recv[:, columns].T
            else:
                far_lean[pl.ds((tile - 5) * LANES, LANES), :] = recv[:, columns].T
        if part == 1:
            for j in range(4):
                spare[pl.ds(j, REST, stride=4), :] = pltpu.roll(rest_recv[...], (LANES - j * REST) % LANES, 1)
            far_lean[pl.ds(4 * LANES, LANES), :] = spare[...].T

    def relay(n):
        for partner in beside:
            pl.semaphore_signal(round_sem.at[n], inc=1, device_id=(partner,), device_id_type=MESH)

    def relayed(n):
        pl.semaphore_wait(round_sem.at[n], len(beside))

    pl.semaphore_wait(barrier, expected)
    tell(low.at[0], along_z, heard_z, 0)
    exchange(0)
    relay(0)

    pack((2, 3))
    thin()
    offer(range(5, TILES))
    offer_rest()
    relayed(0)
    relay(1)

    def interior(ref, normal, change):
        def row_tile(t, carry):
            rows = pl.ds(pl.multiple_of(t * 8, 8), 8)

            def load(c, j):
                return ref[c, j, rows, :]

            def advance(j, carried):
                left, left_flux, left_speed, before = carried
                upper, right = cell_sides(load, j + 1)
                right_flux, right_speed = physical(right, normal)
                flux = interface(left, left_flux, left_speed, right, right_flux, right_speed)
                for c in range(NF):
                    change[c, j - 2, rows, :] = flux[c] - before[c]
                upper_flux, upper_speed = physical(upper, normal)
                return upper, upper_flux, upper_speed, flux

            first, _ = cell_sides(load, 3)
            first_flux, first_speed = physical(first, normal)
            zero = jnp.zeros((8, LANES), F32)
            carried = advance(3, (first, first_flux, first_speed, [zero] * NF))
            last = lax.fori_loop(4, 32, advance, carried, unroll=4)
            for c in range(NF):
                change[c, 0, rows, :] = zero
                change[c, 30, rows, :] = -last[3][c]
                change[c, 31, rows, :] = zero
            return carry

        lax.fori_loop(0, 4, row_tile, 0)

    low[1] = jnp.minimum(low[0], hear(heard_z, 0))
    tell(low.at[1], ends_z, heard_ends, 1)
    for part in (1, 2):
        exchange(part)
    relayed(1)
    relay(2)

    interior(px, 1, cx)
    relayed(2)
    relay(3)
    interior(py, 2, cy)

    low[2] = jnp.minimum(low[1], hear(heard_ends, 1))
    relayed(3)
    tell(low.at[2], plane, heard_plane, 2)

    def corners():
        for face in (2, 3):
            for c in range(NF):
                row = (face * NF + c) * ROWS
                west, east = c * ROWS, (NF + c) * ROWS
                west0, east0 = c * 16, (NF + c) * 16
                for g in range(2):
                    side = g if face == 2 else 31 - g
                    for t, source in ((0, west), (1, west + 32), (30, east + 32), (31, east)):
                        far[pl.ds(row + 32 * g + t, 1), :] = far[pl.ds(source + side, 1), :]
                side = 1 if face == 2 else 14
                far[pl.ds(row + 64, 1), :] = far0[pl.ds(west0 + side, 1), :]
                far[pl.ds(row + 65, 1), :] = far[pl.ds(west + 64 + side, 1), :]
                far[pl.ds(row + 78, 1), :] = far[pl.ds(east + 64 + side, 1), :]
                far[pl.ds(row + 79, 1), :] = far0[pl.ds(east0 + side, 1), :]

    def fatten(face):
        for c in range(NF):
            row = (face * NF + c) * ROWS
            for g in range(2):
                far[pl.ds(row + 32 * g + 2, 28), :] = far_lean[pl.ds((face - 2) * 256 + (2 * c + g) * 28, 28), :]
            far[pl.ds(row + 66, 8), :] = far_lean[pl.ds((face - 2) * 256 + 224 + 8 * c, 8), :]
            far[pl.ds(row + 74, 4), :] = far_lean[pl.ds(512 + (face - 2) * 16 + 4 * c, 4), :]

    def shallow(face):
        for c in range(NF):
            row = (face * NF + c) * ROWS
            far0[pl.ds((face * NF + c) * 16, 16), :] = restricted(far, row, row + 32)

    ghosts = ghost_maker(own, own0, far, far0, relation_v, half_v, near_v, edge, coarse)

    def into(ref):
        def store(c, j, value):
            ref[c, j] = value

        return store

    def apply_x(c, i, change):
        cx[c, i] = cx[c, i] + change

    def join(n, carry):
        low_x, low_y = pl.multiple_of(n // 4 * 8, 8), pl.multiple_of(lax.rem(n, 4) * 8, 8)
        for c in range(NF):
            turned = jnp.swapaxes(cy[c, pl.ds(low_y, 8), pl.ds(low_x, 8), :], 0, 1)
            at = (c, pl.ds(low_x, 8), pl.ds(low_y, 8))
            cx[at] = cx[at] + turned
        return carry

    lax.fori_loop(0, 16, join, 0)

    arrived(0)
    shallow(0)
    ghosts(1, into(px))
    rim(lambda c, j: px[c, j], 1, 1, apply_x)
    def apply_y(c, j, change):
        rows = pl.ds(c * CELLS * CELLS + j, CELLS, stride=CELLS)
        cx2[rows, :] = cx2[rows, :] + change

    arrived(1)
    shallow(1)
    ghosts(0, into(px))
    rim(lambda c, j: px[c, j], 1, 0, apply_x)
    corners()
    fatten(2)
    shallow(2)
    ghosts(3, into(py))
    rim(lambda c, j: py[c, j], 2, 3, apply_y)

    lowest = jnp.minimum(low[2], hear(heard_plane, 2))
    time_step = COURANT * jnp.min(lowest, axis=1, keepdims=True)
    step_out[...] = jnp.broadcast_to(time_step, (1, LANES))
    ratio_out[...] = 0.5 * (time_step / spacing)
    ratio = jnp.broadcast_to(ratio_out[...], (CELLS, LANES))

    def settle(i, carry):
        for c in range(NF):
            out[c, i] = px[c, i + 2] - ratio * cx[c, i]
        return carry

    lax.fori_loop(0, CELLS, settle, 0, unroll=2)

    for stage, slots in enumerate((heard_z, heard_ends, heard_plane)):
        pltpu.make_async_copy(slots, slots, low_send.at[stage]).wait()

    for k in range(NSLOT):

        @pl.when(within(curve[k]))
        def _():
            block = rest_send.at[pl.ds(2 * k, 2)]
            pltpu.make_async_copy(block, block, rest_sem_send.at[k]).wait()

    arrived(2)
    fatten(3)
    shallow(3)
    for k in range(NSLOT):

        @pl.when(within(curve[k]))
        def _():
            block = send.at[pl.ds(k * SEND, SEND)]
            pltpu.make_async_copy(block, block, bulk_send.at[k]).wait()


def deliver(advanced, step, ratio, py, own, own0, far, far0, relation_v, half_v, near_v, out, step_out,
            one, south, turn, outer, edge, coarse, sem):
    copies = [
        pltpu.make_async_copy(advanced.at[c, :, pl.ds(8, 24)], out.at[c, :, pl.ds(8, 24)], sem.at[c])
        for c in range(NF)
    ]
    for copy in copies:
        copy.start()
    one[...] = step[:, pl.ds(0, 1)]
    copies.append(pltpu.make_async_copy(one, step_out, sem.at[2 * NF]))
    copies[-1].start()

    def store(c, j, value):
        outer[c, j] = value

    def load(c, j):
        return outer[c, j] if j < 2 else py[c, j]

    def keep(c, j, change):
        turn[c, j] = change

    ghost_maker(own, own0, far, far0, relation_v, half_v, near_v, edge, coarse)(2, store)
    rim(load, 2, 2, keep)
    for c in range(NF):
        turn[c, pl.ds(2, 6)] = jnp.zeros((6, CELLS, LANES), F32)
        for n in range(4):
            rows = pl.ds(8 * n, 8)
            south[c, rows] = advanced[c, rows, pl.ds(0, 8)] - ratio[...] * jnp.swapaxes(turn[c, :, rows, :], 0, 1)
        copies.append(pltpu.make_async_copy(south.at[c], out.at[c, :, pl.ds(0, 8)], sem.at[NF + c]))
        copies[-1].start()
    for copy in copies:
        copy.wait()


def on_device(fields, patch_level, relation, face_half, neighbour, send_list):
    any_space = pl.BlockSpec(memory_space=pl.ANY)
    vmem = pl.BlockSpec(memory_space=pltpu.VMEM)
    cube = (NF, CELLS, CELLS, LANES)
    held = (
        pltpu.VMEM(cube, F32),
        pltpu.VMEM((1, LANES), F32),
        pltpu.VMEM((1, LANES), F32),
        pltpu.VMEM((NF, PLANES, CELLS, LANES), F32),
        pltpu.VMEM((16 * ROWS, LANES), F32),
        pltpu.VMEM((256, LANES), F32),
        pltpu.VMEM((16 * ROWS, LANES), F32),
        pltpu.VMEM((256, LANES), F32),
        pltpu.VMEM((4, LANES), jnp.int32),
        pltpu.VMEM((4, LANES), jnp.int32),
        pltpu.VMEM((4, 2, LANES), jnp.int32),
    )
    results = pl.pallas_call(
        body,
        out_shape=held,
        in_specs=[any_space] * 6,
        out_specs=(vmem,) * len(held),
        scratch_shapes=[
            pltpu.VMEM((NF, PLANES, CELLS, LANES), F32),
            pltpu.VMEM(cube, F32),
            pltpu.VMEM(cube, F32),
            pltpu.VMEM((1, LANES), jnp.int32),
            pltpu.VMEM((SEND, NSLOT), jnp.int32),
            pltpu.VMEM((5 * LANES, LANES), F32),
            pltpu.VMEM((5 * LANES, LANES), F32),
            pltpu.VMEM((LANES, LANES), F32),
            pltpu.VMEM((LANES, TILES * LANES), F32),
            pltpu.VMEM((LANES, TILES * LANES), F32),
            pltpu.VMEM((REST, LANES), F32),
            pltpu.VMEM((REST, LANES), F32),
            pltpu.VMEM((48, LANES), F32),
            pltpu.VMEM((CELLS, LANES), F32),
            pltpu.VMEM((3, 1, LANES), F32),
            pltpu.VMEM((2 * NEAR_Z, 1, LANES), F32),
            pltpu.VMEM((2, 1, LANES), F32),
            pltpu.VMEM((2 * DIM_X * DIM_Y - 1, 1, LANES), F32),
            pltpu.SemaphoreType.DMA((2 * NF,)),
            pltpu.SemaphoreType.DMA((NF,)),
            pltpu.SemaphoreType.DMA((5,)),
            pltpu.SemaphoreType.DMA((NSLOT,)),
            pltpu.SemaphoreType.DMA((len(PARTS), NSLOT)),
            pltpu.SemaphoreType.DMA((NSLOT,)),
            pltpu.SemaphoreType.DMA((NSLOT,)),
            pltpu.SemaphoreType.DMA((3,)),
            pltpu.SemaphoreType.DMA((3,)),
            pltpu.SemaphoreType.REGULAR((4,)),
        ],
        compiler_params=pltpu.CompilerParams(
            collective_id=0, has_side_effects=True, vmem_limit_bytes=48 << 20
        ),
    )(*(
        pltpu.with_memory_space_constraint(operand, pltpu.HBM)
        for operand in (
            fields,
            patch_level.reshape(1, LANES),
            relation.T,
            face_half.T,
            jnp.transpose(neighbour, (1, 2, 0)),
            send_list[0].T,
        )
    ))
    advanced, step = pl.pallas_call(
        deliver,
        out_shape=(jax.ShapeDtypeStruct(cube, F32), jax.ShapeDtypeStruct((1, 1), F32)),
        in_specs=[vmem] * len(held),
        out_specs=(any_space, any_space),
        scratch_shapes=[
            pltpu.VMEM((1, 1), F32),
            pltpu.VMEM((NF, CELLS, 8, LANES), F32),
            pltpu.VMEM((NF, 8, CELLS, LANES), F32),
            pltpu.VMEM((NF, 2, CELLS, LANES), F32),
            pltpu.VMEM((48, LANES), F32),
            pltpu.VMEM((CELLS, LANES), F32),
            pltpu.SemaphoreType.DMA((2 * NF + 1,)),
        ],
        compiler_params=pltpu.CompilerParams(vmem_limit_bytes=48 << 20),
    )(*(pltpu.with_memory_space_constraint(result, pltpu.VMEM) for result in results))
    return advanced, step.reshape(())


def solution(mesh):
    return jax.shard_map(
        on_device,
        mesh=mesh,
        in_specs=(
            P(None, None, None, "patch"),
            P("patch"),
            P("patch", None),
            P("patch", None),
            P("patch", None, None),
            P("patch", None, None),
        ),
        out_specs=(P(None, None, None, "patch"), P()),
        check_vma=False,
    )
```
